32 devices in a mesh: seq: 8 (over y, x, core), head: 4 (over z).
Axes of the slice: x: 2, y: 2, z: 4, core: 2. Of those that a mesh axis runs over, the one named last changes fastest.
Arguments:
- inputs: bfloat16 [2048, 4096], P('seq'), may hold values from -6 to 6
- x_weight: bfloat16 [4096, 8192], P('seq', 'head'), may hold values from -0.125 to 0.125
- b_values: bfloat16 [2048, 8, 128], P('seq'), may hold values from -0.5 to 0.5
- c_values: bfloat16 [2048, 8, 128], P('seq'), may hold values from -0.375 to 0.375
- gate_z: bfloat16 [2048, 8192], P('seq', 'head'), may hold values from -6 to 6
- log_decay: float32 [2048, 128], P('seq', 'head'), may hold values from -2 to 0
- skip_gain: float32 [128], P('head'), may hold values from 0.5 to 1.5
- grad_out: bfloat16 [2048, 8192], P('seq', 'head'), may hold values from -6 to 6
Outputs:
- input_grad: bfloat16 [2048, 4096], P('seq', 'head')
- z_grad: bfloat16 [2048, 8192], P('seq', 'head')
The draws below stay inside these ranges and needn't reach their ends.
All inputs are finite; a program needn't handle non-finite values.
Results may differ from the reference program's by a relative error of at most 0.0095.
Values may be sent and summed in bfloat16 or wider, within the bound.
A program may use at most 128 MiB of HBM per device.

```python
import jax
import jax.numpy as jnp
from jax import lax

D = 4096
HEADS = 128
HEAD_DIM = 64
STATE = 128
GROUPS = 8
SPAN = 256
SEQLEN = 2048
N_HEAD = 4


def draw_log_decay(key, part):
    keys = jax.random.split(jax.random.fold_in(key, 17), 6)
    slow = jax.random.randint(keys[0], (HEADS,), 0, 2) == 1
    slow_rate = jax.random.uniform(keys[1], (HEADS,), jnp.float32, 0.2, 0.6) / SEQLEN
    fast_rate = jax.random.uniform(keys[2], (HEADS,), jnp.float32, 16.0, 24.0) / SPAN
    rates = jnp.where(slow, slow_rate, fast_rate)
    jitter = jax.random.uniform(keys[3], (SEQLEN, HEADS), jnp.float32, 0.5, 1.5)
    spots = jax.random.randint(keys[4], (3,), 0, SEQLEN)
    hits = jnp.sum((jnp.arange(SEQLEN)[:, None] == spots[None, :]).astype(jnp.float32), axis=1)
    hits = jnp.minimum(hits, 1.0)
    losses = jax.random.uniform(keys[5], (SEQLEN, HEADS), jnp.float32, 0.22, 0.51)
    return -(rates[None, :] * jitter + hits[:, None] * losses)


def spiked(drawn, rng, source, target, shards_of, factor):
    def block_of(axis_at):
        return (jnp.arange(drawn.shape[axis_at]) // (drawn.shape[axis_at] // shards_of)).reshape((-1,) + (1,) * (drawn.ndim - 1 - axis_at))

    first = jax.random.permutation(rng, shards_of)[block_of(target)]
    second = (block_of(target) + shards_of // 2) % shards_of
    return jnp.where((block_of(source) == first) | (block_of(source) == second), factor * drawn, drawn)


def block_levels(stream_key, extent, cuts, smallest, largest):
    loudness, own = 1.0, jax.random.fold_in(stream_key, 6)
    for axis_at, parts in cuts:
        draws = jnp.exp(jax.random.uniform(jax.random.fold_in(own, axis_at), (parts,), jnp.float32, smallest / len(cuts), largest / len(cuts)))
        loudness = loudness * jnp.repeat(draws, extent[axis_at] // parts).reshape([-1 if axis == axis_at else 1 for axis in range(len(extent))])
    return loudness


def bell_draw(stream_key, dims, width, most, shards=(), kind=jnp.bfloat16):
    result = width * jax.random.normal(stream_key, dims, jnp.float32)
    if shards:
        result = result * block_levels(stream_key, dims, shards, -0.22, 0.18)
    return jnp.clip(result, -most, most).astype(kind)


def heavy_noise(stream_key, dims, scale, bound, cuts, heavy, dtype=jnp.bfloat16):
    drawn = scale * jax.random.normal(stream_key, dims, jnp.float32)
    if cuts:
        drawn = drawn * block_levels(stream_key, dims, cuts, -0.22, 0.18)
    return jnp.clip(spiked(drawn, jax.random.fold_in(stream_key, 3), *heavy), -bound, bound).astype(dtype)


def setup_inputs(seed: int = 0) -> dict:
    streams_of = jax.random.split(jax.random.key(seed), 9)
    inputs = bell_draw(streams_of[0], (SEQLEN, D), 1.0, 6.0, ((0, 8),))
    x_weight = heavy_noise(streams_of[1], (D, HEADS * HEAD_DIM), D ** -0.5, 0.125, ((0, 8), (1, 4)), (1, 0, 8, 2.0))
    b_values = bell_draw(streams_of[2], (SEQLEN, GROUPS, STATE), STATE ** -0.5, 0.5, ((0, 8),))
    c_values = bell_draw(streams_of[3], (SEQLEN, GROUPS, STATE), SPAN ** -0.5, 0.375, ((0, 8),))
    gate_z = bell_draw(streams_of[4], (SEQLEN, HEADS * HEAD_DIM), 1.0, 6.0, ((0, 8), (1, 4)))
    log_decay = draw_log_decay(jax.random.fold_in(streams_of[8], 71), 0)
    skip_gain = jnp.clip(0.5 + 1.0 * jax.random.uniform(streams_of[6], (HEADS,), jnp.float32) ** block_levels(streams_of[6], (HEADS,), ((0, 4),), -0.2, 0.2), 0.5, 1.5)
    grad_out = bell_draw(streams_of[7], (SEQLEN, HEADS * HEAD_DIM), 1.0, 6.0, ((0, 8), (1, 4)))
    return {"inputs": inputs, "x_weight": x_weight, "b_values": b_values, "c_values": c_values, "gate_z": gate_z, "log_decay": log_decay, "skip_gain": skip_gain, "grad_out": grad_out}


EXACT_MODE = lax.Precision.HIGHEST


def expand_groups(values):
    return jnp.repeat(values, HEADS // GROUPS, axis=1)


def decayed_scores(c_block, b_block, prefix):
    scores = jnp.einsum('thn,shn->hts', c_block.astype(jnp.float32), b_block.astype(jnp.float32), precision=EXACT_MODE)
    later = prefix.T[:, :, None]
    earlier = prefix.T[:, None, :]
    positions = jnp.arange(prefix.shape[0])
    causal = (positions[:, None] >= positions[None, :])[None, :, :]
    spacing = jnp.where(causal, later - earlier, 0.0)
    factors = jnp.where(causal, jnp.exp(spacing), 0.0)
    return (scores * factors).astype(jnp.bfloat16)


def reference(inputs, x_weight, b_values, c_values, gate_z, log_decay, skip_gain, grad_out):
    block_count = SEQLEN // SPAN
    x_values = jnp.dot(inputs, x_weight, preferred_element_type=jnp.float32).astype(jnp.bfloat16)
    x_blocks = x_values.reshape(block_count, SPAN, HEADS, HEAD_DIM)
    b_blocks = expand_groups(b_values).reshape(block_count, SPAN, HEADS, STATE)
    c_blocks = expand_groups(c_values).reshape(block_count, SPAN, HEADS, STATE)
    decay_blocks = log_decay.reshape(block_count, SPAN, HEADS)
    gate = gate_z.astype(jnp.float32).reshape(SEQLEN, HEADS, HEAD_DIM)
    upstream = grad_out.astype(jnp.float32).reshape(SEQLEN, HEADS, HEAD_DIM)
    sigma = jax.nn.sigmoid(gate)
    y_grad = upstream * gate * sigma
    grad_blocks = y_grad.reshape(block_count, SPAN, HEADS, HEAD_DIM)
    low_blocks = grad_blocks.astype(jnp.bfloat16)
    gain = skip_gain[None, :, None]

    def forward(state, items):
        x_block, b_block, c_block, decay_block = items
        prefix = jnp.cumsum(decay_block, axis=0)
        weights = decayed_scores(c_block, b_block, prefix)
        local = jnp.einsum('hts,shp->thp', weights.astype(jnp.float32), x_block.astype(jnp.float32), precision=EXACT_MODE)
        carried = jnp.exp(prefix)[:, :, None] * jnp.einsum('thn,hpn->thp', c_block.astype(jnp.float32), state, precision=EXACT_MODE)
        tails = jnp.exp(prefix[-1][None, :] - prefix)
        fresh = jnp.einsum('shp,shn->hpn', x_block.astype(jnp.float32) * tails[:, :, None], b_block.astype(jnp.float32), precision=EXACT_MODE)
        state = jnp.exp(prefix[-1])[:, None, None] * state + fresh
        return state, local + carried + gain * x_block.astype(jnp.float32)

    zero_state = jnp.zeros((HEADS, HEAD_DIM, STATE), jnp.float32)
    final_state, outputs = lax.scan(forward, zero_state, (x_blocks, b_blocks, c_blocks, decay_blocks))
    outputs = outputs.reshape(SEQLEN, HEADS, HEAD_DIM)
    z_grad = (upstream * outputs * sigma * (1.0 + gate * (1.0 - sigma))).astype(jnp.bfloat16)
    z_grad = z_grad.reshape(SEQLEN, HEADS * HEAD_DIM)

    def backward(carry, items):
        b_block, c_block, decay_block, grad_block, low_block = items
        prefix = jnp.cumsum(decay_block, axis=0)
        weights = decayed_scores(c_block, b_block, prefix)
        local = jnp.einsum('hts,thp->shp', weights.astype(jnp.float32), low_block.astype(jnp.float32), precision=EXACT_MODE)
        tails = jnp.exp(prefix[-1][None, :] - prefix)
        carried = tails[:, :, None] * jnp.einsum('shn,hpn->shp', b_block.astype(jnp.float32), carry, precision=EXACT_MODE)
        fresh = jnp.einsum('thp,thn->hpn', grad_block * jnp.exp(prefix)[:, :, None], c_block.astype(jnp.float32), precision=EXACT_MODE)
        carry = jnp.exp(prefix[-1])[:, None, None] * carry + fresh
        return carry, local + carried + gain * grad_block

    final_grad, x_grads = lax.scan(backward, zero_state, (b_blocks, c_blocks, decay_blocks, grad_blocks, low_blocks), reverse=True)
    x_grad = x_grads.reshape(SEQLEN, HEADS * HEAD_DIM).astype(jnp.bfloat16)
    group_width = HEADS // N_HEAD * HEAD_DIM
    total_sum = jnp.zeros((SEQLEN, D), jnp.float32)
    for group in range(N_HEAD):
        grad_part = x_grad[:, group * group_width:(group + 1) * group_width]
        weight_part = x_weight[:, group * group_width:(group + 1) * group_width]
        partial_low = jnp.dot(grad_part, weight_part.T, preferred_element_type=jnp.float32).astype(jnp.bfloat16)
        partial_low = lax.optimization_barrier(partial_low)
        total_sum = total_sum + partial_low.astype(jnp.float32)
    input_grad = total_sum.astype(jnp.bfloat16)
    return input_grad, z_grad
```

```python
import jax
import jax.numpy as jnp
from jax import lax
from jax.sharding import PartitionSpec as P
from jax.experimental import pallas as pl
from jax.experimental.pallas import tpu as pltpu

HEADS = 128
HEAD_DIM = 64
STATE = 128
GROUPS = 8
SPAN = 256


EXACT_MODE = lax.Precision.HIGHEST


def prefix_2(array, axis, combine, identity):
    size, place = (lax.axis_size(axis), lax.axis_index(axis))
    everything = jax.tree.map(
        lambda part, kind: lax.all_gather(part.astype(kind), axis),
        array,
        (jnp.bfloat16, jnp.bfloat16),
    )
    start = jax.tree.map(
        lambda part, zero: jnp.broadcast_to(jnp.asarray(zero, part.dtype), part.shape),
        array,
        identity,
    )

    def prefix_hop(k, before):
        reached = k < place
        new = combine(
            before, jax.tree.map(lambda part, own: part[k].astype(own.dtype), everything, array)
        )
        return jax.tree.map(lambda a, b: jnp.where(reached, a, b), new, before)

    return lax.fori_loop(0, size, prefix_hop, start)


def entering(value, axis, join, neutral):
    count, mine = (lax.axis_size(axis), lax.axis_index(axis))
    pieces = jax.tree.map(lambda part: lax.all_gather(part, axis), value)
    pieces = jax.tree.map(lambda part: part[::-1], pieces)
    mine = count - 1 - mine
    so_far = jax.tree.map(
        lambda part, zero: jnp.full_like(part, 0) + jnp.asarray(zero, part.dtype), value, neutral
    )

    def entering_hop(position, so_far):
        longer = join(so_far, jax.tree.map(lambda part: part[position], pieces))
        return jax.tree.map(lambda new, old: jnp.where(position < mine, new, old), longer, so_far)

    return lax.fori_loop(0, count - 1, entering_hop, so_far)


def decayed_scores(c_block, b_block, prefix):
    scores = jnp.einsum("thn,shn->hts", c_block, b_block, preferred_element_type=jnp.float32)
    later = prefix.T[:, :, None]
    earlier = prefix.T[:, None, :]
    positions = jnp.arange(prefix.shape[0])
    causal = (positions[:, None] >= positions[None, :])[None, :, :]
    spacing = jnp.where(causal, later - earlier, 0.0)
    factors = jnp.where(causal, jnp.exp(spacing), 0.0)
    return (scores * factors).astype(jnp.bfloat16)


def compose(earlier, later):
    return (earlier[0] * later[0], later[0][:, None, None] * earlier[1] + later[1])


def body(inputs, x_weight, b_values, c_values, gate_z, log_decay, skip_gain, grad_out):
    token_count = inputs.shape[0]
    head_count = log_decay.shape[1]
    width_here = x_weight.shape[1]
    block_count = token_count // SPAN
    full_weight = lax.all_gather(x_weight, "seq", axis=0, tiled=True)
    x_sums = jnp.dot(inputs, full_weight, preferred_element_type=jnp.float32)
    x_values = x_sums.astype(jnp.bfloat16)
    first_head = lax.axis_index("head") * head_count
    owners = (first_head + jnp.arange(head_count)) // (HEADS // GROUPS)
    picker = (owners[:, None] == jnp.arange(GROUPS)[None, :]).astype(jnp.bfloat16)
    b_heads = jnp.einsum(
        "tgn,hg->thn", b_values, picker, preferred_element_type=jnp.float32
    ).astype(jnp.bfloat16)
    c_heads = jnp.einsum(
        "tgn,hg->thn", c_values, picker, preferred_element_type=jnp.float32
    ).astype(jnp.bfloat16)
    x_blocks = x_values.reshape(block_count, SPAN, head_count, HEAD_DIM)
    b_blocks = b_heads.reshape(block_count, SPAN, head_count, STATE)
    c_blocks = c_heads.reshape(block_count, SPAN, head_count, STATE)
    spots = jnp.arange(SPAN)
    so_far = (spots[:, None] >= spots[None, :]).astype(jnp.float32)
    prefix = jnp.einsum(
        "tr,krh->kth", so_far, log_decay.reshape(block_count, SPAN, head_count), precision=EXACT_MODE
    )
    totals = prefix[:, -1, :]
    gate = gate_z.astype(jnp.float32).reshape(token_count, head_count, HEAD_DIM)
    upstream = grad_out.astype(jnp.float32).reshape(token_count, head_count, HEAD_DIM)
    sigma = jax.nn.sigmoid(gate)
    y_grad = upstream * gate * sigma
    grad_blocks = y_grad.reshape(block_count, SPAN, head_count, HEAD_DIM)
    low_blocks = grad_blocks.astype(jnp.bfloat16)
    tails = jnp.exp(totals[:, None, :] - prefix)
    fresh_states = jnp.einsum(
        "kshp,kshn->khpn",
        x_blocks.astype(jnp.float32) * tails[..., None],
        b_blocks.astype(jnp.float32),
        precision=EXACT_MODE,
    )
    fresh_grads = jnp.einsum(
        "kthp,kthn->khpn",
        grad_blocks * jnp.exp(prefix)[..., None],
        c_blocks.astype(jnp.float32),
        precision=EXACT_MODE,
    )
    blocks = jnp.arange(block_count)
    up_to = (blocks[:, None] >= blocks[None, :]).astype(jnp.float32)
    running = jnp.einsum("jk,kh->jh", up_to, totals, precision=EXACT_MODE)
    after = running[-1][None, :] - running
    before = running - totals
    device_decay = jnp.exp(running[-1])
    device_state = jnp.einsum("kh,khpn->hpn", jnp.exp(after), fresh_states, precision=EXACT_MODE)
    device_grad = jnp.einsum("kh,khpn->hpn", jnp.exp(before), fresh_grads, precision=EXACT_MODE)
    unit_decay = jnp.ones((head_count,), jnp.float32)
    start_state = prefix_2(
        (device_decay, device_state), "seq", compose, (unit_decay, jnp.zeros_like(device_state))
    )[1]
    end_grad = entering(
        (device_decay, device_grad), "seq", compose, (unit_decay, jnp.zeros_like(device_grad))
    )[1]
    gain = skip_gain[None, :, None]

    def forward(state, items):
        x_block, b_block, c_block, prefix_block, fresh = items
        weights = decayed_scores(c_block, b_block, prefix_block)
        local = jnp.einsum("hts,shp->thp", weights, x_block, preferred_element_type=jnp.float32)
        carried = jnp.exp(prefix_block)[:, :, None] * jnp.einsum(
            "thn,hpn->thp", c_block.astype(jnp.float32), state, precision=EXACT_MODE
        )
        state = jnp.exp(prefix_block[-1])[:, None, None] * state + fresh
        return (state, (local + carried + gain * x_block.astype(jnp.float32), weights))

    final_state, (outputs, weight_blocks) = lax.scan(
        forward, start_state, (x_blocks, b_blocks, c_blocks, prefix, fresh_states)
    )
    outputs = outputs.reshape(token_count, head_count, HEAD_DIM)
    z_grad = (upstream * outputs * sigma * (1.0 + gate * (1.0 - sigma))).astype(jnp.bfloat16)
    z_grad = z_grad.reshape(token_count, width_here)

    def backward(carry, items):
        weights, b_block, tail_block, total_block, grad_block, low_block, fresh = items
        local = jnp.einsum("hts,thp->shp", weights, low_block, preferred_element_type=jnp.float32)
        carried = tail_block[:, :, None] * jnp.einsum(
            "shn,hpn->shp", b_block.astype(jnp.float32), carry, precision=EXACT_MODE
        )
        carry = jnp.exp(total_block)[:, None, None] * carry + fresh
        return (carry, local + carried + gain * grad_block)

    final_grad, x_grads = lax.scan(
        backward,
        end_grad,
        (weight_blocks, b_blocks, tails, totals, grad_blocks, low_blocks, fresh_grads),
        reverse=True,
    )
    x_grad = x_grads.reshape(token_count, width_here).astype(jnp.bfloat16)
    partial_sums = jnp.einsum("tk,dk->td", x_grad, full_weight, preferred_element_type=jnp.float32)
    input_grad = lax.psum_scatter(
        partial_sums.astype(jnp.bfloat16), "head", scatter_dimension=1, tiled=True
    )
    return (input_grad, z_grad)


SEQ = 8
RUNS = 4
F32 = jnp.float32
BF16 = jnp.bfloat16


def dot_nn(a, b):
    return lax.dot_general(a, b, (((1,), (0,)), ((), ())), preferred_element_type=F32)


def dot_nt(a, b):
    return lax.dot_general(a, b, (((1,), (1,)), ((), ())), preferred_element_type=F32)


def dot_tn(a, b):
    return lax.dot_general(a, b, (((0,), (0,)), ((), ())), preferred_element_type=F32)


def exact_nn(a, b):
    return lax.dot_general(a, b, (((1,), (0,)), ((), ())), preferred_element_type=F32, precision=EXACT_MODE)


def exact_nt(a, b):
    return lax.dot_general(a, b, (((1,), (1,)), ((), ())), preferred_element_type=F32, precision=EXACT_MODE)


def mixer_kernel(
    in_hbm, w_hbm, b_hbm, c_hbm, gz_hbm, go_hbm, decay_ref, skip_ref,
    out_ref, zg_ref,
    inputs, gz, go, ball, call, b2, c2, pexp, prow, gain,
    wbuf, xacc, xg, xg16, ysc, wts, gmat, x16, pbuf, rin, rdir,
    fbuf, fpart, comp, xr, yt, yr, st, give, tt, tp, csum, cx,
    loads, wsend, wrecv, wlocal, tsend, trecv, esend, erecv, rsend, rrecv, rdrecv,
):
    s = lax.axis_index("seq")
    z = lax.axis_index("head")
    core, xx, yy = s % 2, (s // 2) % 2, s // 4
    depth = w_hbm.shape[0]
    half = depth // 2
    wide = w_hbm.shape[1] // 2
    heads = wts.shape[0]
    pairs = heads // 2
    groups = b2.shape[0]
    per_group = pairs // groups
    per = heads // 4

    def peer(r):
        a = (1 - core) if r & 1 else core
        b = (1 - xx) if r & 2 else xx
        c = (1 - yy) if r & 4 else yy
        return c * 4 + b * 2 + a

    def peer_dyn(r):
        a = (core + r) % 2
        b = (xx + r // 2) % 2
        c = (yy + r // 4) % 2
        return c * 4 + b * 2 + a

    def remote(src, dst, ssem, rsem, to):
        return pltpu.make_async_remote_copy(
            src_ref=src, dst_ref=dst, send_sem=ssem, recv_sem=rsem,
            device_id={"seq": peer(to)}, device_id_type=pl.DeviceIdType.MESH)

    staged = [pltpu.make_async_copy(src, dst, loads.at[n]) for n, (src, dst) in enumerate(
        ((gz_hbm, gz), (go_hbm, go), (c_hbm, call), (b_hbm, ball), (in_hbm, inputs)))]
    for cp in staged:
        cp.start()
    barrier = pltpu.get_barrier_semaphore()
    for r in (1, 2, 4):
        pl.semaphore_signal(barrier, inc=1, device_id={"seq": peer(r)}, device_id_type=pl.DeviceIdType.MESH)
    for dz in range(1, RUNS):
        pl.semaphore_signal(barrier, inc=1, device_id={"head": (z + dz) % RUNS}, device_id_type=pl.DeviceIdType.MESH)
    pl.semaphore_wait(barrier, 3 + RUNS - 1)

    def rows_of(h):
        return pl.ds(h * half, half)

    def wcopy(src_slot, dst_slot, a, h, to):
        if src_slot == 0:
            src = w_hbm.at[rows_of(h), pl.ds(a * wide, wide)]
        else:
            src = wbuf.at[src_slot, a, rows_of(h), :]
        return remote(src, wbuf.at[dst_slot, a, rows_of(h), :],
                      wsend.at[dst_slot, a, h], wrecv.at[dst_slot, a, h], to)

    own = [pltpu.make_async_copy(w_hbm.at[:, pl.ds(a * wide, wide)], wbuf.at[0, a], wlocal.at[a]) for a in range(2)]
    sent = []

    def w_send(src_slot, dst_slot, a, h, to):
        cp = wcopy(src_slot, dst_slot, a, h, to)
        cp.start()
        sent.append(cp)

    def w_wait(slot, a, h, to):
        wcopy(0, slot, a, h, to).wait_recv()

    w_send(0, 2, 0, 0, 2)
    w_send(0, 4, 0, 1, 4)
    for cp in own:
        cp.start()
    for a in range(2):
        for h in range(2):
            w_send(0, 1, a, h, 1)

    lower = (lax.broadcasted_iota(jnp.int32, (SPAN, SPAN), 0) >= lax.broadcasted_iota(jnp.int32, (SPAN, SPAN), 1))
    ones = jnp.where(lower, 1.0, 0.0).astype(F32)
    prefix = exact_nt(ones, decay_ref[...])
    across = exact_nt(decay_ref[...], ones)
    tt[...] = jnp.broadcast_to(across[:, SPAN - 1:SPAN], (heads, 128))
    tcore = remote(tt, tp, tsend.at[0], trecv.at[0], 1)
    tcore.start()
    for i in range(pairs):
        prow[i, 0:2, :] = across[2 * i:2 * i + 2, :]
    both = jnp.concatenate([prefix, jnp.broadcast_to(skip_ref[...], (8, heads))], axis=0)

    lanes = lax.broadcasted_iota(jnp.int32, (SPAN, 128), 1)
    left = lanes < HEAD_DIM
    causal = lax.broadcasted_iota(jnp.int32, (SPAN, SPAN), 0) >= lax.broadcasted_iota(jnp.int32, (SPAN, SPAN), 1)

    def columns_of(i):
        return pl.ds(pl.multiple_of(i * 128, 128), 128)

    staged[0].wait()
    staged[1].wait()

    def prepare_pair(i, carry):
        cols = columns_of(i)
        head = lax.broadcasted_iota(jnp.int32, (heads, 128), 0)
        lane = lax.broadcasted_iota(jnp.int32, (heads, 128), 1)
        pick = jnp.where(head == 2 * i + lane // HEAD_DIM, 1.0, 0.0).astype(F32)
        spread = exact_nn(both, pick)
        pe = spread[:SPAN]
        pexp[i] = pe
        gain[i] = spread[SPAN:]
        gate = gz[:, cols].astype(F32)
        grad = go[:, cols].astype(F32) * gate * jax.nn.sigmoid(gate)
        xg[:, cols] = grad
        ysc[:, cols] = (grad * jnp.exp(pe)).astype(BF16)
        return carry

    lax.fori_loop(0, pairs, prepare_pair, 0)

    some = SPAN // GROUPS
    row = lax.broadcasted_iota(jnp.int32, (groups * some, SPAN), 0)
    col = lax.broadcasted_iota(jnp.int32, (groups * some, SPAN), 1)
    chooser = jnp.where(col == (row % some) * GROUPS + z * groups + row // some, 1.0, 0.0).astype(BF16)

    def choose(src, dst):
        def one(k, carry):
            block = src[pl.ds(pl.multiple_of(k * SPAN, SPAN), SPAN), :]
            chosen = dot_nn(chooser, block).astype(BF16)
            for g in range(groups):
                dst[g, pl.ds(pl.multiple_of(k * some, some), some), :] = chosen[g * some:(g + 1) * some]
            return carry

        lax.fori_loop(0, GROUPS, one, 0)

    staged[2].wait()
    choose(call, c2)

    def fresh(e, a, src, maps):
        def one(j, carry):
            cols = pl.ds(pl.multiple_of(j * 256, 256), 256)
            rows = pl.ds(pl.multiple_of((j % 2) * 256, 256), 256)
            fbuf[e, a, (j // 2) % 2, rows, :] = dot_tn(src[:, cols], maps[j // (SEQ // groups)]).astype(BF16)
            return carry

        lax.fori_loop(4 * a, 4 * a + 4, one, 0)

    def f_copy(e, a):
        return remote(fbuf.at[e, a, 1 - core], fpart.at[e, a], esend.at[0, e, a], erecv.at[0, e, a], 1)

    def x_copy(e, a):
        return remote(comp.at[e, a], xr.at[e, a], esend.at[1, e, a], erecv.at[1, e, a], 2)

    def y_copy(e, a):
        return remote(yt.at[e, a], yr.at[e, a], esend.at[2, e, a], erecv.at[2, e, a], 4)

    def s_copy(e, a):
        return remote(give.at[e, a], st.at[e, a, core], esend.at[3, e, a], erecv.at[3, e, a], 1)

    def s_arrival(e, a):
        return remote(give.at[e, a], st.at[e, a, 1 - core], esend.at[3, e, a], erecv.at[3, e, a], 1)

    def places(e):
        if e == 1:
            return core == 0, xx == 0, yy == 0
        return core == 1, xx == 1, yy == 1

    def decays(ref, a):
        first = a * 2 * per + core * per
        return jnp.exp(ref[pl.ds(pl.multiple_of(first, per), per), :])

    def each_head(one):
        for m in range(per):
            one(m, slice(m * HEAD_DIM, (m + 1) * HEAD_DIM))

    def chip_term(e, a):
        f_copy(e, a).wait_recv()
        early = places(e)[0]
        d = jnp.where(early, decays(tp, a), decays(tt, a))

        def one(m, rows):
            mine = fbuf[e, a, core, rows, :].astype(F32)
            other = fpart[e, a, rows, :].astype(F32)
            comp[e, a, rows, :] = (
                jnp.where(early, other, mine) + d[m:m + 1, :] * jnp.where(early, mine, other)).astype(BF16)

        each_head(one)
        x_copy(e, a).start()

    def row_term(e, a):
        x_copy(e, a).wait_recv()
        _, early, first = places(e)
        d = jnp.where(early, decays(cx, a), decays(csum, a))

        def one(m, rows):
            mine = comp[e, a, rows, :].astype(F32)
            other = xr[e, a, rows, :].astype(F32)
            yt[e, a, rows, :] = (
                jnp.where(early, other, mine) + d[m:m + 1, :] * jnp.where(early, mine, other)).astype(BF16)

        each_head(one)

        @pl.when(first)
        def _():
            y_copy(e, a).start()

    def enter(e, a):
        ahead, early, first = places(e)

        @pl.when(first)
        def _():
            yr[e, a] = jnp.zeros(yr.shape[2:], BF16)

        @pl.when(jnp.logical_not(first))
        def _():
            y_copy(e, a).wait_recv()

        d_row = jnp.where(early, 1.0, decays(cx, a))
        d_core = jnp.where(ahead, decays(tt, a), decays(tp, a))

        def one(m, rows):
            before = jnp.where(early, 0.0, xr[e, a, rows, :].astype(F32))
            reach = before + d_row[m:m + 1, :] * yr[e, a, rows, :].astype(F32)
            mine = fbuf[e, a, core, rows, :].astype(F32)
            other = fpart[e, a, rows, :].astype(F32)
            past = d_core[m:m + 1, :] * reach + jnp.where(ahead, mine, other)
            st[e, a, core, rows, :] = jnp.where(ahead, reach, past).astype(BF16)
            give[e, a, rows, :] = jnp.where(ahead, past, reach).astype(BF16)

        each_head(one)
        s_copy(e, a).start()

    for a in range(2):
        fresh(0, a, ysc, c2)
        f_copy(0, a).start()
    staged[3].wait()
    choose(ball, b2)
    for g in range(groups):
        gmat[g] = dot_nt(c2[g], b2[g])
    tcore.wait_recv()
    csum[...] = tt[...] + tp[...]
    tchip = remote(csum, cx, tsend.at[1], trecv.at[1], 2)
    tchip.start()
    for a in range(2):
        chip_term(0, a)
    w_send(0, 2, 0, 1, 2)
    w_send(0, 4, 0, 0, 4)
    w_wait(2, 0, 0, 2)
    w_send(2, 3, 0, 0, 1)
    w_wait(4, 0, 1, 4)
    w_send(4, 5, 0, 1, 1)
    w_send(4, 6, 0, 1, 2)

    def back_pair(i, carry):
        cols = columns_of(i)
        grad = xg[:, cols]
        low = grad.astype(BF16)
        pe = pexp[i]
        scores = gmat[i // per_group]
        acc = []
        for k in range(2):
            later = pe[:, HEAD_DIM * k:HEAD_DIM * k + 1]
            earlier = prow[i, k:k + 1, :]
            factors = jnp.exp(jnp.where(causal, later - earlier, -1e30))
            w = (scores * factors).astype(BF16)
            wts[2 * i + k] = w
            acc.append(dot_tn(w, low))
        xg[:, cols] = jnp.where(left, acc[0], acc[1]) + gain[i, 0:1, :] * grad
        return carry

    lax.fori_loop(0, pairs, back_pair, 0)
    tchip.wait_recv()
    for a in range(2):
        row_term(0, a)
    w_send(2, 6, 0, 0, 4)
    w_send(0, 4, 1, 1, 4)
    w_send(0, 2, 1, 0, 2)

    def shard_of(slot):
        return inputs[:, pl.ds(pl.multiple_of(peer(slot) * depth, depth), depth)]

    def x_part(slots, a):
        def one(q, carry):
            cs = pl.ds(pl.multiple_of(q * 512, 512), 512)
            total = dot_nn(shard_of(slots[0]), wbuf[slots[0], a, :, cs])
            for slot in slots[1:]:
                total += dot_nn(shard_of(slot), wbuf[slot, a, :, cs])
            into = pl.ds(pl.multiple_of(a * wide + q * 512, 512), 512)
            if slots[0] == 0:
                xacc[:, into] = total
            else:
                xacc[:, into] += total
            return carry

        lax.fori_loop(0, wide // 512, one, 0)

    def route(i):
        target = peer_dyn(i // 2) // 2
        up = (z + RUNS - 1 - target) // RUNS
        return target, up, up * (RUNS - 1)

    def rcopy(i, up):
        return pltpu.make_async_remote_copy(
            src_ref=pbuf.at[i], dst_ref=rin.at[up, i - 12],
            send_sem=rsend.at[i], recv_sem=rrecv.at[up, i - 12],
            device_id={"head": (z + 1 + up * 2) % RUNS}, device_id_type=pl.DeviceIdType.MESH)

    def dcopy(i, source, target):
        return pltpu.make_async_remote_copy(
            src_ref=pbuf.at[i], dst_ref=rdir.at[source, i % 4],
            send_sem=rsend.at[i], recv_sem=rdrecv.at[source, i % 4],
            device_id={"head": target}, device_id_type=pl.DeviceIdType.MESH)

    def p_some(count, index, far):
        def one(k, carry):
            i = index(k)
            slot, h = i // 2, i % 2
            target, up, edge = route(i)
            rows = pl.ds(pl.multiple_of(h * half, half), half)
            total = dot_nt(xg16[:, 0:wide], wbuf[slot, 0, rows, :]) + dot_nt(xg16[:, wide:2 * wide], wbuf[slot, 1, rows, :])
            pbuf[i] = total.astype(BF16)
            if far:
                @pl.when((target != z) & (z == edge))
                def _():
                    rcopy(i, up).start()
            else:
                @pl.when(target != z)
                def _():
                    dcopy(i, z, target).start()

            return carry

        lax.fori_loop(0, count, one, 0)

    def p_pass(first, count):
        def one(i, carry):
            target, up, edge = route(i)

            @pl.when((target != z) & (z != edge))
            def _():
                rcopy(i, up).wait_recv()
                pbuf[i] = (pbuf[i].astype(F32) + rin[up, i - 12].astype(F32)).astype(BF16)
                rcopy(i, up).start()

            return carry

        lax.fori_loop(first, first + count, one, 0)

    def state_of(e, i):
        return st[e, i // 8, (i // 4) % 2, pl.ds(pl.multiple_of((i % 4) * 128, 128), 128), :]

    staged[4].wait()
    for a in range(2):
        own[a].wait()
        for h in range(2):
            w_wait(1, a, h, 1)
        x_part((0, 1), a)
    w_wait(4, 0, 0, 4)
    w_send(4, 5, 0, 0, 1)
    for a in range(2):
        enter(0, a)
    w_wait(2, 0, 1, 2)
    w_send(2, 3, 0, 1, 1)
    for a in range(2):
        s_arrival(0, a).wait_recv()
    w_send(0, 4, 1, 0, 4)

    def back_finish(i, carry):
        cols = columns_of(i)
        pe = pexp[i]
        tail = jnp.exp(pe[SPAN - 1:SPAN, :] - pe)
        xg16[:, cols] = (xg[:, cols] + tail * dot_nt(b2[i // per_group], state_of(0, i))).astype(BF16)
        return carry

    lax.fori_loop(0, pairs, back_finish, 0)
    p_some(4, lambda k: k, False)
    x_part((2, 4), 0)
    for h in range(2):
        w_wait(3, 0, h, 1)
        w_wait(5, 0, h, 1)
    x_part((3, 5), 0)
    w_wait(6, 0, 0, 4)
    w_send(6, 7, 0, 0, 1)
    w_wait(6, 0, 1, 2)
    w_send(6, 7, 0, 1, 1)
    x_part((6,), 0)
    w_wait(7, 0, 0, 1)
    w_wait(7, 0, 1, 1)
    x_part((7,), 0)

    def fore_scale(a):
        def one(i, carry):
            cols = columns_of(i)
            x = xacc[:, cols].astype(BF16)
            x16[:, cols] = x
            pe = pexp[i]
            ysc[:, cols] = (x.astype(F32) * jnp.exp(pe[SPAN - 1:SPAN, :] - pe)).astype(BF16)
            return carry

        lax.fori_loop(pairs // 2 * a, pairs // 2 * (a + 1), one, 0)

    def fore_local(a):
        def one(i, carry):
            cols = columns_of(i)
            x = x16[:, cols]
            y = jnp.where(left, dot_nn(wts[2 * i], x), dot_nn(wts[2 * i + 1], x))
            xacc[:, cols] = y + gain[i, 0:1, :] * x.astype(F32)
            return carry

        lax.fori_loop(pairs // 2 * a, pairs // 2 * (a + 1), one, 0)

    def fore_finish(a):
        def one(i, carry):
            cols = columns_of(i)
            y = xacc[:, cols] + jnp.exp(pexp[i]) * dot_nt(c2[i // per_group], state_of(1, i))
            gate = gz[:, cols].astype(F32)
            up = go[:, cols].astype(F32)
            sigma = jax.nn.sigmoid(gate)
            zg_ref[:, cols] = (up * y * sigma * (1.0 + gate * (1.0 - sigma))).astype(BF16)
            return carry

        lax.fori_loop(pairs // 2 * a, pairs // 2 * (a + 1), one, 0)

    fore_scale(0)
    fresh(1, 0, ysc, b2)
    f_copy(1, 0).start()
    chip_term(1, 0)
    w_send(0, 2, 1, 1, 2)
    fore_local(0)
    w_wait(2, 1, 0, 2)
    w_send(2, 3, 1, 0, 1)
    w_wait(4, 1, 1, 4)
    w_send(4, 5, 1, 1, 1)
    w_send(4, 6, 1, 1, 2)
    row_term(1, 0)
    w_send(2, 6, 1, 0, 4)
    w_wait(3, 1, 0, 1)
    w_wait(5, 1, 1, 1)
    p_some(4, lambda k: 4 + 2 * k + k // 2, False)
    w_wait(2, 1, 1, 2)
    w_send(2, 3, 1, 1, 1)
    w_wait(4, 1, 0, 4)
    w_send(4, 5, 1, 0, 1)
    x_part((2, 4), 1)
    w_wait(3, 1, 1, 1)
    w_wait(5, 1, 0, 1)
    p_some(4, lambda k: 5 + 2 * k - k // 2, False)
    x_part((3, 5), 1)
    enter(1, 0)
    s_arrival(1, 0).wait_recv()
    fore_finish(0)
    w_wait(6, 1, 0, 4)
    w_send(6, 7, 1, 0, 1)
    w_wait(6, 1, 1, 2)
    w_send(6, 7, 1, 1, 1)
    x_part((6,), 1)
    p_some(2, lambda k: 12 + k, True)
    w_wait(7, 1, 0, 1)
    w_wait(7, 1, 1, 1)
    x_part((7,), 1)
    fore_scale(1)
    fresh(1, 1, ysc, b2)
    f_copy(1, 1).start()
    p_some(2, lambda k: 14 + k, True)
    chip_term(1, 1)
    p_pass(12, 2)
    fore_local(1)
    row_term(1, 1)
    p_pass(14, 2)
    enter(1, 1)
    s_arrival(1, 1).wait_recv()
    fore_finish(1)

    def own_chunk(i, far):
        owner = peer_dyn(i // 2)

        @pl.when(owner // 2 == z)
        def _():
            piece = (owner % 2) * 2 + i % 2
            out_cols = pl.ds(pl.multiple_of(piece * 256, 256), 256)
            xg[:, out_cols] = pbuf[i].astype(F32)
            if far:
                @pl.when(z != 0)
                def _():
                    rcopy(i, 0).wait_recv()
                    xg[:, out_cols] += rin[0, i - 12].astype(F32)

                @pl.when(z != RUNS - 1)
                def _():
                    rcopy(i, 1).wait_recv()
                    xg[:, out_cols] += rin[1, i - 12].astype(F32)
            else:
                for dz in range(1, RUNS):
                    source = (z + dz) % RUNS
                    dcopy(i, source, source).wait_recv()
                    xg[:, out_cols] += rdir[source, i % 4].astype(F32)
            out_ref[:, out_cols] = xg[:, out_cols].astype(BF16)

    def own_near(i, carry):
        own_chunk(i, False)
        return carry

    def own_far(i, carry):
        own_chunk(i, True)
        return carry

    lax.fori_loop(0, 12, own_near, 0)
    lax.fori_loop(12, 16, own_far, 0)

    def drain(i, carry):
        target = route(i)[0]

        @pl.when(target != z)
        def _():
            dcopy(i, z, target).wait_send()

        return carry

    lax.fori_loop(0, 16, drain, 0)
    for cp in sent:
        cp.wait_send()
    tcore.wait_send()
    tchip.wait_send()
    for e in range(2):
        for a in range(2):
            f_copy(e, a).wait_send()
            x_copy(e, a).wait_send()
            s_copy(e, a).wait_send()

            @pl.when(places(e)[2])
            def _():
                y_copy(e, a).wait_send()


def fused_body(inputs, x_weight, b_values, c_values, gate_z, log_decay, skip_gain, grad_out):
    heads = log_decay.shape[1]
    width = x_weight.shape[1]
    depth = x_weight.shape[0]
    pairs = heads // 2
    groups = heads * GROUPS // HEADS
    tokens = inputs.shape[0]
    b_rows = b_values.reshape(tokens * GROUPS, STATE)
    c_rows = c_values.reshape(tokens * GROUPS, STATE)
    vmem = pl.BlockSpec(memory_space=pltpu.VMEM)
    hbm = pl.BlockSpec(memory_space=pl.ANY)
    dma = pltpu.SemaphoreType.DMA
    part = pltpu.VMEM((2, 2, heads // 4 * HEAD_DIM, STATE), BF16)
    parts = pltpu.VMEM((2, 2, 2, heads // 4 * HEAD_DIM, STATE), BF16)
    total = pltpu.VMEM((heads, 128), F32)
    return tuple(pl.pallas_call(
        mixer_kernel,
        out_shape=(
            pltpu.VMEM((tokens, inputs.shape[1] // RUNS), BF16),
            pltpu.VMEM((tokens, width), BF16),
        ),
        in_specs=[hbm, hbm, hbm, hbm, hbm, hbm, vmem, vmem],
        out_specs=(vmem, vmem),
        scratch_shapes=[
            pltpu.VMEM(inputs.shape, BF16),
            pltpu.VMEM((tokens, width), BF16),
            pltpu.VMEM((tokens, width), BF16),
            pltpu.VMEM(b_rows.shape, BF16),
            pltpu.VMEM(b_rows.shape, BF16),
            pltpu.VMEM((groups, SPAN, STATE), BF16),
            pltpu.VMEM((groups, SPAN, STATE), BF16),
            pltpu.VMEM((pairs, SPAN, 128), F32),
            pltpu.VMEM((pairs, 8, SPAN), F32),
            pltpu.VMEM((pairs, 8, 128), F32),
            pltpu.VMEM((SEQ, 2, depth, width // 2), BF16),
            pltpu.VMEM((tokens, width), F32),
            pltpu.VMEM((tokens, width), F32),
            pltpu.VMEM((tokens, width), BF16),
            pltpu.VMEM((tokens, width), BF16),
            pltpu.VMEM((heads, SPAN, SPAN), BF16),
            pltpu.VMEM((groups, SPAN, SPAN), F32),
            pltpu.VMEM((tokens, width), BF16),
            pltpu.VMEM((2 * SEQ, tokens, depth // 2), BF16),
            pltpu.VMEM((2, 4, tokens, depth // 2), BF16),
            pltpu.VMEM((RUNS, 4, tokens, depth // 2), BF16),
            parts, part, part, part, part, part, parts, part,
            total, total, total, total,
            dma((5,)), dma((SEQ, 2, 2)), dma((SEQ, 2, 2)), dma((2,)),
            dma((2,)), dma((2,)),
            dma((4, 2, 2)), dma((4, 2, 2)),
            dma((2 * SEQ,)), dma((2, 4)), dma((RUNS, 4)),
        ],
        compiler_params=pltpu.CompilerParams(
            collective_id=0, has_side_effects=True, vmem_limit_bytes=60 * 1024 * 1024),
        name="mixer",
    )(inputs, x_weight, b_rows, c_rows, gate_z, grad_out, log_decay.T, skip_gain[None, :]))


def solution(mesh):
    in_specs = (
        P("seq", None),
        P("seq", "head"),
        P("seq", None, None),
        P("seq", None, None),
        P("seq", "head"),
        P("seq", "head"),
        P("head"),
        P("seq", "head"),
    )
    out_specs = (P("seq", "head"), P("seq", "head"))
    small = mesh.shape["seq"] == SEQ and mesh.shape["head"] == RUNS
    chosen = fused_body if small else body
    return jax.shard_map(chosen, mesh=mesh, in_specs=in_specs, out_specs=out_specs, check_vma=False)
```

```python
import jax
import jax.numpy as jnp
from jax import lax
from jax.sharding import PartitionSpec as P
from jax.experimental import pallas as pl
from jax.experimental.pallas import tpu as pltpu

HEADS = 128
HEAD_DIM = 64
STATE = 128
GROUPS = 8
SPAN = 256


EXACT_MODE = lax.Precision.HIGHEST


def prefix_2(array, axis, combine, identity):
    size, place = (lax.axis_size(axis), lax.axis_index(axis))
    everything = jax.tree.map(
        lambda part, kind: lax.all_gather(part.astype(kind), axis),
        array,
        (jnp.bfloat16, jnp.bfloat16),
    )
    start = jax.tree.map(
        lambda part, zero: jnp.broadcast_to(jnp.asarray(zero, part.dtype), part.shape),
        array,
        identity,
    )

    def prefix_hop(k, before):
        reached = k < place
        new = combine(
            before, jax.tree.map(lambda part, own: part[k].astype(own.dtype), everything, array)
        )
        return jax.tree.map(lambda a, b: jnp.where(reached, a, b), new, before)

    return lax.fori_loop(0, size, prefix_hop, start)


def entering(value, axis, join, neutral):
    count, mine = (lax.axis_size(axis), lax.axis_index(axis))
    pieces = jax.tree.map(lambda part: lax.all_gather(part, axis), value)
    pieces = jax.tree.map(lambda part: part[::-1], pieces)
    mine = count - 1 - mine
    so_far = jax.tree.map(
        lambda part, zero: jnp.full_like(part, 0) + jnp.asarray(zero, part.dtype), value, neutral
    )

    def entering_hop(position, so_far):
        longer = join(so_far, jax.tree.map(lambda part: part[position], pieces))
        return jax.tree.map(lambda new, old: jnp.where(position < mine, new, old), longer, so_far)

    return lax.fori_loop(0, count - 1, entering_hop, so_far)


def decayed_scores(c_block, b_block, prefix):
    scores = jnp.einsum("thn,shn->hts", c_block, b_block, preferred_element_type=jnp.float32)
    later = prefix.T[:, :, None]
    earlier = prefix.T[:, None, :]
    positions = jnp.arange(prefix.shape[0])
    causal = (positions[:, None] >= positions[None, :])[None, :, :]
    spacing = jnp.where(causal, later - earlier, 0.0)
    factors = jnp.where(causal, jnp.exp(spacing), 0.0)
    return (scores * factors).astype(jnp.bfloat16)


def compose(earlier, later):
    return (earlier[0] * later[0], later[0][:, None, None] * earlier[1] + later[1])


def body(inputs, x_weight, b_values, c_values, gate_z, log_decay, skip_gain, grad_out):
    token_count = inputs.shape[0]
    head_count = log_decay.shape[1]
    width_here = x_weight.shape[1]
    block_count = token_count // SPAN
    full_weight = lax.all_gather(x_weight, "seq", axis=0, tiled=True)
    x_sums = jnp.dot(inputs, full_weight, preferred_element_type=jnp.float32)
    x_values = x_sums.astype(jnp.bfloat16)
    first_head = lax.axis_index("head") * head_count
    owners = (first_head + jnp.arange(head_count)) // (HEADS // GROUPS)
    picker = (owners[:, None] == jnp.arange(GROUPS)[None, :]).astype(jnp.bfloat16)
    b_heads = jnp.einsum(
        "tgn,hg->thn", b_values, picker, preferred_element_type=jnp.float32
    ).astype(jnp.bfloat16)
    c_heads = jnp.einsum(
        "tgn,hg->thn", c_values, picker, preferred_element_type=jnp.float32
    ).astype(jnp.bfloat16)
    x_blocks = x_values.reshape(block_count, SPAN, head_count, HEAD_DIM)
    b_blocks = b_heads.reshape(block_count, SPAN, head_count, STATE)
    c_blocks = c_heads.reshape(block_count, SPAN, head_count, STATE)
    spots = jnp.arange(SPAN)
    so_far = (spots[:, None] >= spots[None, :]).astype(jnp.float32)
    prefix = jnp.einsum(
        "tr,krh->kth", so_far, log_decay.reshape(block_count, SPAN, head_count), precision=EXACT_MODE
    )
    totals = prefix[:, -1, :]
    gate = gate_z.astype(jnp.float32).reshape(token_count, head_count, HEAD_DIM)
    upstream = grad_out.astype(jnp.float32).reshape(token_count, head_count, HEAD_DIM)
    sigma = jax.nn.sigmoid(gate)
    y_grad = upstream * gate * sigma
    grad_blocks = y_grad.reshape(block_count, SPAN, head_count, HEAD_DIM)
    low_blocks = grad_blocks.astype(jnp.bfloat16)
    tails = jnp.exp(totals[:, None, :] - prefix)
    fresh_states = jnp.einsum(
        "kshp,kshn->khpn",
        x_blocks.astype(jnp.float32) * tails[..., None],
        b_blocks.astype(jnp.float32),
        precision=EXACT_MODE,
    )
    fresh_grads = jnp.einsum(
        "kthp,kthn->khpn",
        grad_blocks * jnp.exp(prefix)[..., None],
        c_blocks.astype(jnp.float32),
        precision=EXACT_MODE,
    )
    blocks = jnp.arange(block_count)
    up_to = (blocks[:, None] >= blocks[None, :]).astype(jnp.float32)
    running = jnp.einsum("jk,kh->jh", up_to, totals, precision=EXACT_MODE)
    after = running[-1][None, :] - running
    before = running - totals
    device_decay = jnp.exp(running[-1])
    device_state = jnp.einsum("kh,khpn->hpn", jnp.exp(after), fresh_states, precision=EXACT_MODE)
    device_grad = jnp.einsum("kh,khpn->hpn", jnp.exp(before), fresh_grads, precision=EXACT_MODE)
    unit_decay = jnp.ones((head_count,), jnp.float32)
    start_state = prefix_2(
        (device_decay, device_state), "seq", compose, (unit_decay, jnp.zeros_like(device_state))
    )[1]
    end_grad = entering(
        (device_decay, device_grad), "seq", compose, (unit_decay, jnp.zeros_like(device_grad))
    )[1]
    gain = skip_gain[None, :, None]

    def forward(state, items):
        x_block, b_block, c_block, prefix_block, fresh = items
        weights = decayed_scores(c_block, b_block, prefix_block)
        local = jnp.einsum("hts,shp->thp", weights, x_block, preferred_element_type=jnp.float32)
        carried = jnp.exp(prefix_block)[:, :, None] * jnp.einsum(
            "thn,hpn->thp", c_block.astype(jnp.float32), state, precision=EXACT_MODE
        )
        state = jnp.exp(prefix_block[-1])[:, None, None] * state + fresh
        return (state, (local + carried + gain * x_block.astype(jnp.float32), weights))

    final_state, (outputs, weight_blocks) = lax.scan(
        forward, start_state, (x_blocks, b_blocks, c_blocks, prefix, fresh_states)
    )
    outputs = outputs.reshape(token_count, head_count, HEAD_DIM)
    z_grad = (upstream * outputs * sigma * (1.0 + gate * (1.0 - sigma))).astype(jnp.bfloat16)
    z_grad = z_grad.reshape(token_count, width_here)

    def backward(carry, items):
        weights, b_block, tail_block, total_block, grad_block, low_block, fresh = items
        local = jnp.einsum("hts,thp->shp", weights, low_block, preferred_element_type=jnp.float32)
        carried = tail_block[:, :, None] * jnp.einsum(
            "shn,hpn->shp", b_block.astype(jnp.float32), carry, precision=EXACT_MODE
        )
        carry = jnp.exp(total_block)[:, None, None] * carry + fresh
        return (carry, local + carried + gain * grad_block)

    final_grad, x_grads = lax.scan(
        backward,
        end_grad,
        (weight_blocks, b_blocks, tails, totals, grad_blocks, low_blocks, fresh_grads),
        reverse=True,
    )
    x_grad = x_grads.reshape(token_count, width_here).astype(jnp.bfloat16)
    partial_sums = jnp.einsum("tk,dk->td", x_grad, full_weight, preferred_element_type=jnp.float32)
    input_grad = lax.psum_scatter(
        partial_sums.astype(jnp.bfloat16), "head", scatter_dimension=1, tiled=True
    )
    return (input_grad, z_grad)


SEQ = 8
RUNS = 4
F32 = jnp.float32
BF16 = jnp.bfloat16


def dot_nn(a, b):
    return lax.dot_general(a, b, (((1,), (0,)), ((), ())), preferred_element_type=F32)


def dot_nt(a, b):
    return lax.dot_general(a, b, (((1,), (1,)), ((), ())), preferred_element_type=F32)


def dot_tn(a, b):
    return lax.dot_general(a, b, (((0,), (0,)), ((), ())), preferred_element_type=F32)


def exact_nn(a, b):
    return lax.dot_general(a, b, (((1,), (0,)), ((), ())), preferred_element_type=F32, precision=EXACT_MODE)


def exact_nt(a, b):
    return lax.dot_general(a, b, (((1,), (1,)), ((), ())), preferred_element_type=F32, precision=EXACT_MODE)


def mixer_kernel(
    in_hbm, w_hbm, b_hbm, c_hbm, gz_hbm, go_hbm, decay_ref, skip_ref,
    out_ref, zg_ref,
    inputs, gz, go, ball, call, b2, c2, pexp, prow, gain,
    wbuf, xacc, xg, xg16, ysc, wts, gmat, x16, zfac, pbuf, rin, rdir,
    fbuf, fpart, comp, xr, yt, yr, st, give, tt, tp, csum, cx,
    loads, wsend, wrecv, wlocal, tsend, trecv, esend, erecv, rsend, rrecv, rdrecv,
):
    s = lax.axis_index("seq")
    z = lax.axis_index("head")
    core, xx, yy = s % 2, (s // 2) % 2, s // 4
    depth = w_hbm.shape[0]
    half = depth // 2
    fine = half // 4
    wide = w_hbm.shape[1] // 2
    heads = wts.shape[0]
    pairs = heads // 2
    groups = b2.shape[0]
    per_group = pairs // groups
    per = heads // 8
    quarters = range(4)

    def peer(r):
        a = (1 - core) if r & 1 else core
        b = (1 - xx) if r & 2 else xx
        c = (1 - yy) if r & 4 else yy
        return c * 4 + b * 2 + a

    def peer_dyn(r):
        a = (core + r) % 2
        b = (xx + r // 2) % 2
        c = (yy + r // 4) % 2
        return c * 4 + b * 2 + a

    def remote(src, dst, ssem, rsem, to):
        return pltpu.make_async_remote_copy(
            src_ref=src, dst_ref=dst, send_sem=ssem, recv_sem=rsem,
            device_id={"seq": peer(to)}, device_id_type=pl.DeviceIdType.MESH)

    staged = [pltpu.make_async_copy(src, dst, loads.at[n]) for n, (src, dst) in enumerate(
        ((gz_hbm, gz), (go_hbm, go), (c_hbm, call), (b_hbm, ball), (in_hbm, inputs)))]
    for cp in staged:
        cp.start()
    barrier = pltpu.get_barrier_semaphore()
    for r in (1, 2, 4):
        pl.semaphore_signal(barrier, inc=1, device_id={"seq": peer(r)}, device_id_type=pl.DeviceIdType.MESH)
    for dz in range(1, RUNS):
        pl.semaphore_signal(barrier, inc=1, device_id={"head": (z + dz) % RUNS}, device_id_type=pl.DeviceIdType.MESH)
    pl.semaphore_wait(barrier, 3 + RUNS - 1)

    def rows_of(h, sub):
        if sub is None:
            return pl.ds(h * half, half)
        return pl.ds(h * half + sub * fine, fine)

    def wcopy(src_slot, dst_slot, a, h, to, sub=None):
        rows = rows_of(h, sub)
        if src_slot == 0:
            src = w_hbm.at[rows, pl.ds(a * wide, wide)]
        else:
            src = wbuf.at[src_slot, a, rows, :]
        return remote(src, wbuf.at[dst_slot, a, rows, :],
                      wsend.at[dst_slot, a, h, sub or 0], wrecv.at[dst_slot, a, h, sub or 0], to)

    own = [pltpu.make_async_copy(w_hbm.at[:, pl.ds(a * wide, wide)], wbuf.at[0, a], wlocal.at[a]) for a in range(2)]
    sent = []

    def w_send(src_slot, dst_slot, a, h, to, sub=None):
        cp = wcopy(src_slot, dst_slot, a, h, to, sub)
        cp.start()
        sent.append(cp)

    def w_wait(slot, a, h, to, sub=None):
        wcopy(0, slot, a, h, to, sub).wait_recv()

    w_send(0, 2, 0, 0, 2)
    w_send(0, 4, 0, 1, 4)
    w_send(0, 4, 1, 1, 4)
    for cp in own:
        cp.start()
    for a in range(2):
        for h in range(2):
            w_send(0, 1, a, h, 1)

    lower = (lax.broadcasted_iota(jnp.int32, (SPAN, SPAN), 0) >= lax.broadcasted_iota(jnp.int32, (SPAN, SPAN), 1))
    ones = jnp.where(lower, 1.0, 0.0).astype(F32)
    prefix = exact_nt(ones, decay_ref[...])
    across = exact_nt(decay_ref[...], ones)
    tt[...] = jnp.broadcast_to(across[:, SPAN - 1:SPAN], (heads, 128))
    tcore = remote(tt, tp, tsend.at[0], trecv.at[0], 1)
    tcore.start()
    for i in range(pairs):
        prow[i, 0:2, :] = across[2 * i:2 * i + 2, :]
    both = jnp.concatenate([prefix, jnp.broadcast_to(skip_ref[...], (8, heads))], axis=0)

    lanes = lax.broadcasted_iota(jnp.int32, (SPAN, 128), 1)
    left = lanes < HEAD_DIM
    causal = lax.broadcasted_iota(jnp.int32, (SPAN, SPAN), 0) >= lax.broadcasted_iota(jnp.int32, (SPAN, SPAN), 1)

    def columns_of(i):
        return pl.ds(pl.multiple_of(i * 128, 128), 128)

    staged[0].wait()
    staged[1].wait()

    def prepare_pair(i, carry):
        cols = columns_of(i)
        head = lax.broadcasted_iota(jnp.int32, (heads, 128), 0)
        lane = lax.broadcasted_iota(jnp.int32, (heads, 128), 1)
        pick = jnp.where(head == 2 * i + lane // HEAD_DIM, 1.0, 0.0).astype(F32)
        spread = exact_nn(both, pick)
        pe = spread[:SPAN]
        pexp[i] = pe
        gain[i] = spread[SPAN:]
        gate = gz[:, cols].astype(F32)
        grad = go[:, cols].astype(F32) * gate * jax.nn.sigmoid(gate)
        xg[:, cols] = grad
        ysc[:, cols] = (grad * jnp.exp(pe)).astype(BF16)
        return carry

    lax.fori_loop(0, pairs, prepare_pair, 0)

    some = SPAN // GROUPS
    row = lax.broadcasted_iota(jnp.int32, (groups * some, SPAN), 0)
    col = lax.broadcasted_iota(jnp.int32, (groups * some, SPAN), 1)
    chooser = jnp.where(col == (row % some) * GROUPS + z * groups + row // some, 1.0, 0.0).astype(BF16)

    def choose(src, dst):
        def one(k, carry):
            block = src[pl.ds(pl.multiple_of(k * SPAN, SPAN), SPAN), :]
            chosen = dot_nn(chooser, block).astype(BF16)
            for g in range(groups):
                dst[g, pl.ds(pl.multiple_of(k * some, some), some), :] = chosen[g * some:(g + 1) * some]
            return carry

        lax.fori_loop(0, GROUPS, one, 0)

    staged[2].wait()
    choose(call, c2)

    def fresh(e, u, src, maps):
        def one(j, carry):
            cols = pl.ds(pl.multiple_of(j * 256, 256), 256)
            fbuf[e, u, j % 2] = dot_tn(src[:, cols], maps[j // (SEQ // groups)]).astype(BF16)
            return carry

        lax.fori_loop(2 * u, 2 * u + 2, one, 0)

    def f_copy(e, a):
        return remote(fbuf.at[e, a, 1 - core], fpart.at[e, a], esend.at[0, e, a], erecv.at[0, e, a], 1)

    def x_copy(e, a):
        return remote(comp.at[e, a], xr.at[e, a], esend.at[1, e, a], erecv.at[1, e, a], 2)

    def y_copy(e, a):
        return remote(yt.at[e, a], yr.at[e, a], esend.at[2, e, a], erecv.at[2, e, a], 4)

    def s_copy(e, a):
        return remote(give.at[e, a], st.at[e, a, core], esend.at[3, e, a], erecv.at[3, e, a], 1)

    def s_arrival(e, a):
        return remote(give.at[e, a], st.at[e, a, 1 - core], esend.at[3, e, a], erecv.at[3, e, a], 1)

    def places(e):
        if e == 1:
            return core == 0, xx == 0, yy == 0
        return core == 1, xx == 1, yy == 1

    def decays(ref, a):
        both_cores = ref[a * 2 * per:(a + 1) * 2 * per, :]
        return jnp.exp(jnp.where(core == 0, both_cores[:per], both_cores[per:]))

    def each_head(one):
        for m in range(per):
            one(m, slice(m * HEAD_DIM, (m + 1) * HEAD_DIM))

    def chip_term(e, a):
        f_copy(e, a).wait_recv()
        early = places(e)[0]
        d = jnp.where(early, decays(tp, a), decays(tt, a))

        def one(m, rows):
            mine = fbuf[e, a, core, rows, :].astype(F32)
            other = fpart[e, a, rows, :].astype(F32)
            comp[e, a, rows, :] = (
                jnp.where(early, other, mine) + d[m:m + 1, :] * jnp.where(early, mine, other)).astype(BF16)

        each_head(one)
        x_copy(e, a).start()

    def row_term(e, a):
        x_copy(e, a).wait_recv()
        _, early, first = places(e)
        d = jnp.where(early, decays(cx, a), decays(csum, a))

        def one(m, rows):
            mine = comp[e, a, rows, :].astype(F32)
            other = xr[e, a, rows, :].astype(F32)
            yt[e, a, rows, :] = (
                jnp.where(early, other, mine) + d[m:m + 1, :] * jnp.where(early, mine, other)).astype(BF16)

        each_head(one)

        @pl.when(first)
        def _():
            y_copy(e, a).start()

    def enter(e, a):
        ahead, early, first = places(e)

        @pl.when(first)
        def _():
            yr[e, a] = jnp.zeros(yr.shape[2:], BF16)

        @pl.when(jnp.logical_not(first))
        def _():
            y_copy(e, a).wait_recv()

        d_row = jnp.where(early, 1.0, decays(cx, a))
        d_core = jnp.where(ahead, decays(tt, a), decays(tp, a))

        def one(m, rows):
            before = jnp.where(early, 0.0, xr[e, a, rows, :].astype(F32))
            reach = before + d_row[m:m + 1, :] * yr[e, a, rows, :].astype(F32)
            mine = fbuf[e, a, core, rows, :].astype(F32)
            other = fpart[e, a, rows, :].astype(F32)
            past = d_core[m:m + 1, :] * reach + jnp.where(ahead, mine, other)
            st[e, a, core, rows, :] = jnp.where(ahead, reach, past).astype(BF16)
            give[e, a, rows, :] = jnp.where(ahead, past, reach).astype(BF16)

        each_head(one)
        s_copy(e, a).start()

    for u in quarters:
        fresh(0, u, ysc, c2)
        f_copy(0, u).start()
    staged[3].wait()
    choose(ball, b2)
    for g in range(groups):
        gmat[g] = dot_nt(c2[g], b2[g])
    tcore.wait_recv()
    csum[...] = tt[...] + tp[...]
    tchip = remote(csum, cx, tsend.at[1], trecv.at[1], 2)
    tchip.start()
    for u in quarters:
        chip_term(0, u)
    w_send(0, 2, 1, 0, 2)
    w_wait(2, 0, 0, 2)
    w_send(2, 3, 0, 0, 1)
    w_wait(4, 0, 1, 4)
    w_send(4, 5, 0, 1, 1)

    def back_pair(i, carry):
        cols = columns_of(i)
        grad = xg[:, cols]
        low = grad.astype(BF16)
        pe = pexp[i]
        scores = gmat[i // per_group]
        acc = []
        for k in range(2):
            later = pe[:, HEAD_DIM * k:HEAD_DIM * k + 1]
            earlier = prow[i, k:k + 1, :]
            factors = jnp.exp(jnp.where(causal, later - earlier, -1e30))
            w = (scores * factors).astype(BF16)
            wts[2 * i + k] = w
            acc.append(dot_tn(w, low))
        xg[:, cols] = jnp.where(left, acc[0], acc[1]) + gain[i, 0:1, :] * grad
        return carry

    lax.fori_loop(0, pairs, back_pair, 0)
    tchip.wait_recv()
    for u in quarters:
        row_term(0, u)
    w_send(0, 4, 0, 0, 4)
    w_send(0, 2, 0, 1, 2)

    def shard_of(slot):
        return inputs[:, pl.ds(pl.multiple_of(peer(slot) * depth, depth), depth)]

    def x_part(slots, a):
        def one(q, carry):
            cs = pl.ds(pl.multiple_of(q * 512, 512), 512)
            total = dot_nn(shard_of(slots[0]), wbuf[slots[0], a, :, cs])
            for slot in slots[1:]:
                total += dot_nn(shard_of(slot), wbuf[slot, a, :, cs])
            into = pl.ds(pl.multiple_of(a * wide + q * 512, 512), 512)
            if slots[0] == 0:
                xacc[:, into] = total
            else:
                xacc[:, into] += total
            return carry

        lax.fori_loop(0, wide // 512, one, 0)

    def route(i):
        target = peer_dyn(jnp.minimum(i // 2, 6)) // 2
        up = (z + RUNS - 1 - target) // RUNS
        return target, up, up * (RUNS - 1)

    def rcopy(i, up):
        return pltpu.make_async_remote_copy(
            src_ref=pbuf.at[i], dst_ref=rin.at[up, i - 12],
            send_sem=rsend.at[i], recv_sem=rrecv.at[up, i - 12],
            device_id={"head": (z + 1 + up * 2) % RUNS}, device_id_type=pl.DeviceIdType.MESH)

    def dcopy(i, source, target):
        return pltpu.make_async_remote_copy(
            src_ref=pbuf.at[i], dst_ref=rdir.at[source, i % 4],
            send_sem=rsend.at[i], recv_sem=rdrecv.at[source, i % 4],
            device_id={"head": target}, device_id_type=pl.DeviceIdType.MESH)

    def p_send(i, total, far):
        target, up, edge = route(i)
        pbuf[i] = total.astype(BF16)
        if far:
            @pl.when((target != z) & (z == edge))
            def _():
                rcopy(i, up).start()
        else:
            @pl.when(target != z)
            def _():
                dcopy(i, z, target).start()

    def p_some(count, index, far):
        def one(k, carry):
            i = index(k)
            slot, h = i // 2, i % 2
            rows = pl.ds(pl.multiple_of(h * half, half), half)
            total = dot_nt(xg16[:, 0:wide], wbuf[slot, 0, rows, :]) + dot_nt(xg16[:, wide:2 * wide], wbuf[slot, 1, rows, :])
            p_send(i, total, far)
            return carry

        lax.fori_loop(0, count, one, 0)

    def p_diag(sub):
        def picked(a):
            return jnp.concatenate([
                wbuf[slot, a, h * half + sub * fine:h * half + (sub + 1) * fine, :]
                for slot in (6, 7) for h in range(2)], axis=0)

        total = dot_nt(xg16[:, 0:wide], picked(0)) + dot_nt(xg16[:, wide:2 * wide], picked(1))
        p_send(12 + sub, total, True)

    def p_pass(hop, i):
        target, up, edge = route(i)
        away = jnp.where(up == 1, edge - z, z - edge)

        @pl.when((target != z) & (away == hop))
        def _():
            rcopy(i, up).wait_recv()
            pbuf[i] = (pbuf[i].astype(F32) + rin[up, i - 12].astype(F32)).astype(BF16)
            rcopy(i, up).start()

    def group_1(k):
        return 4 + 2 * k + k // 2

    def group_2(k):
        return 5 + 2 * k - k // 2

    def state_of(e, i):
        return st[e, i // 4, (i // 2) % 2, pl.ds(pl.multiple_of((i % 2) * 128, 128), 128), :]

    staged[4].wait()
    for a in range(2):
        own[a].wait()
        for h in range(2):
            w_wait(1, a, h, 1)
        x_part((0, 1), a)

    def z_factor(i, carry):
        cols = columns_of(i)
        gate = gz[:, cols].astype(F32)
        sigma = jax.nn.sigmoid(gate)
        zfac[:, cols] = go[:, cols].astype(F32) * sigma * (1.0 + gate * (1.0 - sigma))
        return carry

    lax.fori_loop(0, pairs, z_factor, 0)
    w_wait(4, 1, 1, 4)
    w_send(4, 5, 1, 1, 1)
    w_wait(2, 1, 0, 2)
    w_send(2, 3, 1, 0, 1)
    w_send(0, 2, 1, 1, 2)
    w_send(0, 4, 1, 0, 4)
    for u in quarters:
        enter(0, u)
    for u in quarters:
        s_arrival(0, u).wait_recv()

    def back_finish(i, carry):
        cols = columns_of(i)
        pe = pexp[i]
        tail = jnp.exp(pe[SPAN - 1:SPAN, :] - pe)
        xg16[:, cols] = (xg[:, cols] + tail * dot_nt(b2[i // per_group], state_of(0, i))).astype(BF16)
        return carry

    lax.fori_loop(0, pairs, back_finish, 0)
    p_some(4, lambda k: k, False)
    w_wait(3, 0, 0, 1)
    w_wait(5, 0, 1, 1)
    w_wait(3, 1, 0, 1)
    w_wait(5, 1, 1, 1)
    p_some(4, group_1, False)
    w_wait(2, 0, 1, 2)
    w_send(2, 3, 0, 1, 1)
    w_send(2, 6, 0, 0, 4)
    w_wait(4, 0, 0, 4)
    w_send(4, 5, 0, 0, 1)
    w_send(4, 6, 0, 1, 2)
    x_part((2, 4), 0)
    w_wait(3, 0, 1, 1)
    w_wait(5, 0, 0, 1)
    x_part((3, 5), 0)

    def fore_scale(u):
        def one(i, carry):
            cols = columns_of(i)
            x = xacc[:, cols].astype(BF16)
            x16[:, cols] = x
            pe = pexp[i]
            ysc[:, cols] = (x.astype(F32) * jnp.exp(pe[SPAN - 1:SPAN, :] - pe)).astype(BF16)
            return carry

        lax.fori_loop(pairs // 4 * u, pairs // 4 * (u + 1), one, 0)

    def fore_local(u):
        def one(i, carry):
            cols = columns_of(i)
            x = x16[:, cols]
            y = jnp.where(left, dot_nn(wts[2 * i], x), dot_nn(wts[2 * i + 1], x))
            xacc[:, cols] = y + gain[i, 0:1, :] * x.astype(F32)
            return carry

        lax.fori_loop(pairs // 4 * u, pairs // 4 * (u + 1), one, 0)

    def fore_finish(u):
        def one(i, carry):
            cols = columns_of(i)
            y = xacc[:, cols] + jnp.exp(pexp[i]) * dot_nt(c2[i // per_group], state_of(1, i))
            zg_ref[:, cols] = (y * zfac[:, cols]).astype(BF16)
            return carry

        lax.fori_loop(pairs // 4 * u, pairs // 4 * (u + 1), one, 0)

    def own_chunk(i, carry):
        owner = peer_dyn(i // 2)

        @pl.when(owner // 2 == z)
        def _():
            total = pbuf[i].astype(F32)
            for dz in range(1, RUNS):
                source = (z + dz) % RUNS
                dcopy(i, source, source).wait_recv()
                total += rdir[source, i % 4].astype(F32)
            piece = (owner % 2) * 2 + i % 2
            out_ref[:, pl.ds(pl.multiple_of(piece * 256, 256), 256)] = total.astype(BF16)

        return carry

    def own_far():
        @pl.when(peer(6) // 2 == z)
        def _():
            for sub in range(4):
                i = 12 + sub
                cols = slice(sub * 256, (sub + 1) * 256)
                xg[:, cols] = pbuf[i].astype(F32)

                @pl.when(z != 0)
                def _():
                    rcopy(i, 0).wait_recv()
                    xg[:, cols] += rin[0, sub].astype(F32)

                @pl.when(z != RUNS - 1)
                def _():
                    rcopy(i, 1).wait_recv()
                    xg[:, cols] += rin[1, sub].astype(F32)

            for slot in (6, 7):
                for h in range(2):
                    for k in range(2):
                        first = (slot - 6) * 128 + h * 64
                        block = jnp.concatenate([
                            xg[:, sub * 256 + first:sub * 256 + first + 64] for sub in (2 * k, 2 * k + 1)], axis=1)
                        place = (peer(slot) % 2) * 4 + h * 2 + k
                        out_ref[:, pl.ds(pl.multiple_of(place * 128, 128), 128)] = block.astype(BF16)

    w_wait(2, 1, 1, 2)
    w_send(2, 3, 1, 1, 1)
    w_wait(4, 1, 0, 4)
    w_send(4, 5, 1, 0, 1)
    for sub in range(2):
        w_send(4, 6, 1, 1, 2, sub)
    for sub in range(4):
        w_send(2, 6, 1, 0, 4, sub)
    x_part((2, 4), 1)
    w_wait(3, 1, 1, 1)
    w_wait(5, 1, 0, 1)
    p_some(4, group_2, False)
    x_part((3, 5), 1)
    w_wait(6, 0, 0, 4)
    w_send(6, 7, 0, 0, 1)
    w_wait(6, 0, 1, 2)
    w_send(6, 7, 0, 1, 1)
    x_part((6,), 0)
    w_wait(7, 0, 0, 1)
    w_wait(7, 0, 1, 1)
    x_part((7,), 0)
    for u in range(2):
        fore_scale(u)
        fresh(1, u, ysc, b2)
        f_copy(1, u).start()
    for u in range(2):
        chip_term(1, u)
    for sub in range(2, 4):
        w_send(4, 6, 1, 1, 2, sub)

    def diag_step(sub):
        w_wait(6, 1, 0, 4, sub)
        w_send(6, 7, 1, 0, 1, sub)
        w_wait(6, 1, 1, 2, sub)
        w_send(6, 7, 1, 1, 1, sub)

    def diag_rest(sub):
        w_wait(7, 1, 0, 1, sub)
        w_wait(7, 1, 1, 1, sub)

    diag_step(0)
    diag_rest(0)
    p_diag(0)
    diag_step(1)
    for u in range(2):
        row_term(1, u)
    diag_rest(1)
    p_diag(1)
    for u in range(2):
        fore_local(u)
    diag_step(2)
    p_pass(1, 12)
    diag_rest(2)
    p_diag(2)
    p_pass(1, 13)
    diag_step(3)
    x_part((6,), 1)
    p_pass(2, 12)
    diag_rest(3)
    x_part((7,), 1)
    for u in range(2, 4):
        fore_scale(u)
        fresh(1, u, ysc, b2)
        f_copy(1, u).start()
    p_diag(3)
    p_pass(1, 14)
    for u in range(2, 4):
        chip_term(1, u)
    p_pass(2, 13)
    for u in range(2):
        enter(1, u)
    for u in range(2, 4):
        fore_local(u)
    p_pass(1, 15)
    for u in range(2):
        s_arrival(1, u).wait_recv()
        fore_finish(u)
    p_pass(2, 14)
    for u in range(2, 4):
        row_term(1, u)
    lax.fori_loop(0, 12, own_chunk, 0)
    p_pass(2, 15)
    for u in range(2, 4):
        enter(1, u)
    for u in range(2, 4):
        s_arrival(1, u).wait_recv()
        fore_finish(u)
    own_far()

    def drain(i, carry):
        target = route(i)[0]

        @pl.when(target != z)
        def _():
            dcopy(i, z, target).wait_send()

        return carry

    lax.fori_loop(0, 16, drain, 0)
    for cp in sent:
        cp.wait_send()
    tcore.wait_send()
    tchip.wait_send()
    for e in range(2):
        for u in quarters:
            f_copy(e, u).wait_send()
            x_copy(e, u).wait_send()
            s_copy(e, u).wait_send()

            @pl.when(places(e)[2])
            def _():
                y_copy(e, u).wait_send()


def fused_body(inputs, x_weight, b_values, c_values, gate_z, log_decay, skip_gain, grad_out):
    heads = log_decay.shape[1]
    width = x_weight.shape[1]
    depth = x_weight.shape[0]
    pairs = heads // 2
    groups = heads * GROUPS // HEADS
    tokens = inputs.shape[0]
    b_rows = b_values.reshape(tokens * GROUPS, STATE)
    c_rows = c_values.reshape(tokens * GROUPS, STATE)
    vmem = pl.BlockSpec(memory_space=pltpu.VMEM)
    hbm = pl.BlockSpec(memory_space=pl.ANY)
    dma = pltpu.SemaphoreType.DMA
    part = pltpu.VMEM((2, 4, heads // 8 * HEAD_DIM, STATE), BF16)
    parts = pltpu.VMEM((2, 4, 2, heads // 8 * HEAD_DIM, STATE), BF16)
    total = pltpu.VMEM((heads, 128), F32)
    return tuple(pl.pallas_call(
        mixer_kernel,
        out_shape=(
            pltpu.VMEM((tokens, inputs.shape[1] // RUNS), BF16),
            pltpu.VMEM((tokens, width), BF16),
        ),
        in_specs=[hbm, hbm, hbm, hbm, hbm, hbm, vmem, vmem],
        out_specs=(vmem, vmem),
        scratch_shapes=[
            pltpu.VMEM(inputs.shape, BF16),
            pltpu.VMEM((tokens, width), BF16),
            pltpu.VMEM((tokens, width), BF16),
            pltpu.VMEM(b_rows.shape, BF16),
            pltpu.VMEM(b_rows.shape, BF16),
            pltpu.VMEM((groups, SPAN, STATE), BF16),
            pltpu.VMEM((groups, SPAN, STATE), BF16),
            pltpu.VMEM((pairs, SPAN, 128), F32),
            pltpu.VMEM((pairs, 8, SPAN), F32),
            pltpu.VMEM((pairs, 8, 128), F32),
            pltpu.VMEM((SEQ, 2, depth, width // 2), BF16),
            pltpu.VMEM((tokens, width), F32),
            pltpu.VMEM((tokens, width), F32),
            pltpu.VMEM((tokens, width), BF16),
            pltpu.VMEM((tokens, width), BF16),
            pltpu.VMEM((heads, SPAN, SPAN), BF16),
            pltpu.VMEM((groups, SPAN, SPAN), F32),
            pltpu.VMEM((tokens, width), BF16),
            pltpu.VMEM((tokens, width), F32),
            pltpu.VMEM((2 * SEQ, tokens, depth // 2), BF16),
            pltpu.VMEM((2, 4, tokens, depth // 2), BF16),
            pltpu.VMEM((RUNS, 4, tokens, depth // 2), BF16),
            parts, part, part, part, part, part, parts, part,
            total, total, total, total,
            dma((5,)), dma((SEQ, 2, 2, 4)), dma((SEQ, 2, 2, 4)), dma((2,)),
            dma((2,)), dma((2,)),
            dma((4, 2, 4)), dma((4, 2, 4)),
            dma((2 * SEQ,)), dma((2, 4)), dma((RUNS, 4)),
        ],
        compiler_params=pltpu.CompilerParams(
            collective_id=0, has_side_effects=True, vmem_limit_bytes=60 * 1024 * 1024),
        name="mixer",
    )(inputs, x_weight, b_rows, c_rows, gate_z, grad_out, log_decay.T, skip_gain[None, :]))


def solution(mesh):
    in_specs = (
        P("seq", None),
        P("seq", "head"),
        P("seq", None, None),
        P("seq", None, None),
        P("seq", "head"),
        P("seq", "head"),
        P("head"),
        P("seq", "head"),
    )
    out_specs = (P("seq", "head"), P("seq", "head"))
    small = mesh.shape["seq"] == SEQ and mesh.shape["head"] == RUNS
    chosen = fused_body if small else body
    return jax.shard_map(chosen, mesh=mesh, in_specs=in_specs, out_specs=out_specs, check_vma=False)
```

```python
import jax
import jax.numpy as jnp
from jax import lax
from jax.sharding import PartitionSpec as P
from jax.experimental import pallas as pl
from jax.experimental.pallas import tpu as pltpu

HEADS = 128
HEAD_DIM = 64
STATE = 128
GROUPS = 8
SPAN = 256


EXACT_MODE = lax.Precision.HIGHEST


def prefix_2(array, axis, combine, identity):
    size, place = (lax.axis_size(axis), lax.axis_index(axis))
    everything = jax.tree.map(
        lambda part, kind: lax.all_gather(part.astype(kind), axis),
        array,
        (jnp.bfloat16, jnp.bfloat16),
    )
    start = jax.tree.map(
        lambda part, zero: jnp.broadcast_to(jnp.asarray(zero, part.dtype), part.shape),
        array,
        identity,
    )

    def prefix_hop(k, before):
        reached = k < place
        new = combine(
            before, jax.tree.map(lambda part, own: part[k].astype(own.dtype), everything, array)
        )
        return jax.tree.map(lambda a, b: jnp.where(reached, a, b), new, before)

    return lax.fori_loop(0, size, prefix_hop, start)


def entering(value, axis, join, neutral):
    count, mine = (lax.axis_size(axis), lax.axis_index(axis))
    pieces = jax.tree.map(lambda part: lax.all_gather(part, axis), value)
    pieces = jax.tree.map(lambda part: part[::-1], pieces)
    mine = count - 1 - mine
    so_far = jax.tree.map(
        lambda part, zero: jnp.full_like(part, 0) + jnp.asarray(zero, part.dtype), value, neutral
    )

    def entering_hop(position, so_far):
        longer = join(so_far, jax.tree.map(lambda part: part[position], pieces))
        return jax.tree.map(lambda new, old: jnp.where(position < mine, new, old), longer, so_far)

    return lax.fori_loop(0, count - 1, entering_hop, so_far)


def decayed_scores(c_block, b_block, prefix):
    scores = jnp.einsum("thn,shn->hts", c_block, b_block, preferred_element_type=jnp.float32)
    later = prefix.T[:, :, None]
    earlier = prefix.T[:, None, :]
    positions = jnp.arange(prefix.shape[0])
    causal = (positions[:, None] >= positions[None, :])[None, :, :]
    spacing = jnp.where(causal, later - earlier, 0.0)
    factors = jnp.where(causal, jnp.exp(spacing), 0.0)
    return (scores * factors).astype(jnp.bfloat16)


def compose(earlier, later):
    return (earlier[0] * later[0], later[0][:, None, None] * earlier[1] + later[1])


def body(inputs, x_weight, b_values, c_values, gate_z, log_decay, skip_gain, grad_out):
    token_count = inputs.shape[0]
    head_count = log_decay.shape[1]
    width_here = x_weight.shape[1]
    block_count = token_count // SPAN
    full_weight = lax.all_gather(x_weight, "seq", axis=0, tiled=True)
    x_sums = jnp.dot(inputs, full_weight, preferred_element_type=jnp.float32)
    x_values = x_sums.astype(jnp.bfloat16)
    first_head = lax.axis_index("head") * head_count
    owners = (first_head + jnp.arange(head_count)) // (HEADS // GROUPS)
    picker = (owners[:, None] == jnp.arange(GROUPS)[None, :]).astype(jnp.bfloat16)
    b_heads = jnp.einsum(
        "tgn,hg->thn", b_values, picker, preferred_element_type=jnp.float32
    ).astype(jnp.bfloat16)
    c_heads = jnp.einsum(
        "tgn,hg->thn", c_values, picker, preferred_element_type=jnp.float32
    ).astype(jnp.bfloat16)
    x_blocks = x_values.reshape(block_count, SPAN, head_count, HEAD_DIM)
    b_blocks = b_heads.reshape(block_count, SPAN, head_count, STATE)
    c_blocks = c_heads.reshape(block_count, SPAN, head_count, STATE)
    spots = jnp.arange(SPAN)
    so_far = (spots[:, None] >= spots[None, :]).astype(jnp.float32)
    prefix = jnp.einsum(
        "tr,krh->kth", so_far, log_decay.reshape(block_count, SPAN, head_count), precision=EXACT_MODE
    )
    totals = prefix[:, -1, :]
    gate = gate_z.astype(jnp.float32).reshape(token_count, head_count, HEAD_DIM)
    upstream = grad_out.astype(jnp.float32).reshape(token_count, head_count, HEAD_DIM)
    sigma = jax.nn.sigmoid(gate)
    y_grad = upstream * gate * sigma
    grad_blocks = y_grad.reshape(block_count, SPAN, head_count, HEAD_DIM)
    low_blocks = grad_blocks.astype(jnp.bfloat16)
    tails = jnp.exp(totals[:, None, :] - prefix)
    fresh_states = jnp.einsum(
        "kshp,kshn->khpn",
        x_blocks.astype(jnp.float32) * tails[..., None],
        b_blocks.astype(jnp.float32),
        precision=EXACT_MODE,
    )
    fresh_grads = jnp.einsum(
        "kthp,kthn->khpn",
        grad_blocks * jnp.exp(prefix)[..., None],
        c_blocks.astype(jnp.float32),
        precision=EXACT_MODE,
    )
    blocks = jnp.arange(block_count)
    up_to = (blocks[:, None] >= blocks[None, :]).astype(jnp.float32)
    running = jnp.einsum("jk,kh->jh", up_to, totals, precision=EXACT_MODE)
    after = running[-1][None, :] - running
    before = running - totals
    device_decay = jnp.exp(running[-1])
    device_state = jnp.einsum("kh,khpn->hpn", jnp.exp(after), fresh_states, precision=EXACT_MODE)
    device_grad = jnp.einsum("kh,khpn->hpn", jnp.exp(before), fresh_grads, precision=EXACT_MODE)
    unit_decay = jnp.ones((head_count,), jnp.float32)
    start_state = prefix_2(
        (device_decay, device_state), "seq", compose, (unit_decay, jnp.zeros_like(device_state))
    )[1]
    end_grad = entering(
        (device_decay, device_grad), "seq", compose, (unit_decay, jnp.zeros_like(device_grad))
    )[1]
    gain = skip_gain[None, :, None]

    def forward(state, items):
        x_block, b_block, c_block, prefix_block, fresh = items
        weights = decayed_scores(c_block, b_block, prefix_block)
        local = jnp.einsum("hts,shp->thp", weights, x_block, preferred_element_type=jnp.float32)
        carried = jnp.exp(prefix_block)[:, :, None] * jnp.einsum(
            "thn,hpn->thp", c_block.astype(jnp.float32), state, precision=EXACT_MODE
        )
        state = jnp.exp(prefix_block[-1])[:, None, None] * state + fresh
        return (state, (local + carried + gain * x_block.astype(jnp.float32), weights))

    final_state, (outputs, weight_blocks) = lax.scan(
        forward, start_state, (x_blocks, b_blocks, c_blocks, prefix, fresh_states)
    )
    outputs = outputs.reshape(token_count, head_count, HEAD_DIM)
    z_grad = (upstream * outputs * sigma * (1.0 + gate * (1.0 - sigma))).astype(jnp.bfloat16)
    z_grad = z_grad.reshape(token_count, width_here)

    def backward(carry, items):
        weights, b_block, tail_block, total_block, grad_block, low_block, fresh = items
        local = jnp.einsum("hts,thp->shp", weights, low_block, preferred_element_type=jnp.float32)
        carried = tail_block[:, :, None] * jnp.einsum(
            "shn,hpn->shp", b_block.astype(jnp.float32), carry, precision=EXACT_MODE
        )
        carry = jnp.exp(total_block)[:, None, None] * carry + fresh
        return (carry, local + carried + gain * grad_block)

    final_grad, x_grads = lax.scan(
        backward,
        end_grad,
        (weight_blocks, b_blocks, tails, totals, grad_blocks, low_blocks, fresh_grads),
        reverse=True,
    )
    x_grad = x_grads.reshape(token_count, width_here).astype(jnp.bfloat16)
    partial_sums = jnp.einsum("tk,dk->td", x_grad, full_weight, preferred_element_type=jnp.float32)
    input_grad = lax.psum_scatter(
        partial_sums.astype(jnp.bfloat16), "head", scatter_dimension=1, tiled=True
    )
    return (input_grad, z_grad)


SEQ = 8
RUNS = 4
F32 = jnp.float32
BF16 = jnp.bfloat16


def dot_nn(a, b):
    return lax.dot_general(a, b, (((1,), (0,)), ((), ())), preferred_element_type=F32)


def dot_nt(a, b):
    return lax.dot_general(a, b, (((1,), (1,)), ((), ())), preferred_element_type=F32)


def dot_tn(a, b):
    return lax.dot_general(a, b, (((0,), (0,)), ((), ())), preferred_element_type=F32)


def exact_nn(a, b):
    return lax.dot_general(a, b, (((1,), (0,)), ((), ())), preferred_element_type=F32, precision=EXACT_MODE)


def exact_nt(a, b):
    return lax.dot_general(a, b, (((1,), (1,)), ((), ())), preferred_element_type=F32, precision=EXACT_MODE)


def mixer_kernel(
    in_hbm, w_hbm, b_hbm, c_hbm, gz_hbm, go_hbm, decay_ref, skip_ref,
    out_ref, zg_ref,
    inputs, gz, go, ball, call, b2, c2, pexp, prow, gain,
    wbuf, xacc, xg, xg16, ysc, wts, gmat, x16, zfac, pbuf, rin, rdir,
    fbuf, fpart, comp, xr, yt, yr, st, give, tt, tp, csum, cx,
    loads, wsend, wrecv, wlocal, tsend, trecv, esend, erecv, rsend, rrecv, rdrecv,
):
    s = lax.axis_index("seq")
    z = lax.axis_index("head")
    core, xx, yy = s % 2, (s // 2) % 2, s // 4
    depth = w_hbm.shape[0]
    half = depth // 2
    fine = half // 4
    wide = w_hbm.shape[1] // 2
    heads = wts.shape[0]
    pairs = heads // 2
    groups = b2.shape[0]
    per_group = pairs // groups
    per = heads // 8
    quarters = range(4)

    def peer(r):
        a = (1 - core) if r & 1 else core
        b = (1 - xx) if r & 2 else xx
        c = (1 - yy) if r & 4 else yy
        return c * 4 + b * 2 + a

    def peer_dyn(r):
        a = (core + r) % 2
        b = (xx + r // 2) % 2
        c = (yy + r // 4) % 2
        return c * 4 + b * 2 + a

    def remote(src, dst, ssem, rsem, to):
        return pltpu.make_async_remote_copy(
            src_ref=src, dst_ref=dst, send_sem=ssem, recv_sem=rsem,
            device_id={"seq": peer(to)}, device_id_type=pl.DeviceIdType.MESH)

    staged = [pltpu.make_async_copy(src, dst, loads.at[n]) for n, (src, dst) in enumerate(
        ((gz_hbm, gz), (go_hbm, go), (c_hbm, call), (b_hbm, ball), (in_hbm, inputs)))]
    for cp in staged:
        cp.start()
    barrier = pltpu.get_barrier_semaphore()
    for r in (1, 2, 4):
        pl.semaphore_signal(barrier, inc=1, device_id={"seq": peer(r)}, device_id_type=pl.DeviceIdType.MESH)
    for dz in range(1, RUNS):
        pl.semaphore_signal(barrier, inc=1, device_id={"head": (z + dz) % RUNS}, device_id_type=pl.DeviceIdType.MESH)
    pl.semaphore_wait(barrier, 3 + RUNS - 1)

    def rows_of(h, sub):
        if sub is None:
            return pl.ds(h * half, half)
        return pl.ds(h * half + sub * fine, fine)

    def wcopy(src_slot, dst_slot, a, h, to, sub=None):
        rows = rows_of(h, sub)
        if src_slot == 0:
            src = w_hbm.at[rows, pl.ds(a * wide, wide)]
        else:
            src = wbuf.at[src_slot, a, rows, :]
        return remote(src, wbuf.at[dst_slot, a, rows, :],
                      wsend.at[dst_slot, a, h, sub or 0], wrecv.at[dst_slot, a, h, sub or 0], to)

    own = [pltpu.make_async_copy(w_hbm.at[:, pl.ds(a * wide, wide)], wbuf.at[0, a], wlocal.at[a]) for a in range(2)]
    sent = []

    def w_send(src_slot, dst_slot, a, h, to, sub=None):
        cp = wcopy(src_slot, dst_slot, a, h, to, sub)
        cp.start()
        sent.append(cp)

    def w_wait(slot, a, h, to, sub=None):
        wcopy(0, slot, a, h, to, sub).wait_recv()

    w_send(0, 2, 0, 0, 2)
    w_send(0, 4, 0, 1, 4)
    w_send(0, 2, 1, 0, 2, 0)
    w_send(0, 4, 1, 1, 4)
    for cp in own:
        cp.start()
    for a in range(2):
        for h in range(2):
            w_send(0, 1, a, h, 1)

    lower = (lax.broadcasted_iota(jnp.int32, (SPAN, SPAN), 0) >= lax.broadcasted_iota(jnp.int32, (SPAN, SPAN), 1))
    ones = jnp.where(lower, 1.0, 0.0).astype(F32)
    prefix = exact_nt(ones, decay_ref[...])
    across = exact_nt(decay_ref[...], ones)
    tt[...] = jnp.broadcast_to(across[:, SPAN - 1:SPAN], (heads, 128))
    tcore = remote(tt, tp, tsend.at[0], trecv.at[0], 1)
    tcore.start()
    for i in range(pairs):
        prow[i, 0:2, :] = across[2 * i:2 * i + 2, :]
    both = jnp.concatenate([prefix, jnp.broadcast_to(skip_ref[...], (8, heads))], axis=0)

    lanes = lax.broadcasted_iota(jnp.int32, (SPAN, 128), 1)
    left = lanes < HEAD_DIM
    causal = lax.broadcasted_iota(jnp.int32, (SPAN, SPAN), 0) >= lax.broadcasted_iota(jnp.int32, (SPAN, SPAN), 1)

    def columns_of(i):
        return pl.ds(pl.multiple_of(i * 128, 128), 128)

    staged[0].wait()
    staged[1].wait()

    def prepare_pair(i, carry):
        cols = columns_of(i)
        head = lax.broadcasted_iota(jnp.int32, (heads, 128), 0)
        lane = lax.broadcasted_iota(jnp.int32, (heads, 128), 1)
        pick = jnp.where(head == 2 * i + lane // HEAD_DIM, 1.0, 0.0).astype(F32)
        spread = exact_nn(both, pick)
        pe = spread[:SPAN]
        pexp[i] = pe
        gain[i] = spread[SPAN:]
        gate = gz[:, cols].astype(F32)
        grad = go[:, cols].astype(F32) * gate * jax.nn.sigmoid(gate)
        xg[:, cols] = grad
        ysc[:, cols] = (grad * jnp.exp(pe)).astype(BF16)
        return carry

    lax.fori_loop(0, pairs, prepare_pair, 0)

    some = SPAN // GROUPS
    row = lax.broadcasted_iota(jnp.int32, (groups * some, SPAN), 0)
    col = lax.broadcasted_iota(jnp.int32, (groups * some, SPAN), 1)
    chooser = jnp.where(col == (row % some) * GROUPS + z * groups + row // some, 1.0, 0.0).astype(BF16)

    def choose(src, dst):
        def one(k, carry):
            block = src[pl.ds(pl.multiple_of(k * SPAN, SPAN), SPAN), :]
            chosen = dot_nn(chooser, block).astype(BF16)
            for g in range(groups):
                dst[g, pl.ds(pl.multiple_of(k * some, some), some), :] = chosen[g * some:(g + 1) * some]
            return carry

        lax.fori_loop(0, GROUPS, one, 0)

    staged[2].wait()
    choose(call, c2)

    def fresh(e, u, src, maps):
        def one(j, carry):
            cols = pl.ds(pl.multiple_of(j * 256, 256), 256)
            fbuf[e, u, j % 2] = dot_tn(src[:, cols], maps[j // (SEQ // groups)]).astype(BF16)
            return carry

        lax.fori_loop(2 * u, 2 * u + 2, one, 0)

    def f_copy(e, a):
        return remote(fbuf.at[e, a, 1 - core], fpart.at[e, a], esend.at[0, e, a], erecv.at[0, e, a], 1)

    def x_copy(e, a):
        return remote(comp.at[e, a], xr.at[e, a], esend.at[1, e, a], erecv.at[1, e, a], 2)

    def y_copy(e, a):
        return remote(yt.at[e, a], yr.at[e, a], esend.at[2, e, a], erecv.at[2, e, a], 4)

    def s_copy(e, a):
        return remote(give.at[e, a], st.at[e, a, core], esend.at[3, e, a], erecv.at[3, e, a], 1)

    def s_arrival(e, a):
        return remote(give.at[e, a], st.at[e, a, 1 - core], esend.at[3, e, a], erecv.at[3, e, a], 1)

    def places(e):
        if e == 1:
            return core == 0, xx == 0, yy == 0
        return core == 1, xx == 1, yy == 1

    def decays(ref, a):
        both_cores = ref[a * 2 * per:(a + 1) * 2 * per, :]
        return jnp.exp(jnp.where(core == 0, both_cores[:per], both_cores[per:]))

    def each_head(one):
        for m in range(per):
            one(m, slice(m * HEAD_DIM, (m + 1) * HEAD_DIM))

    def chip_term(e, a):
        f_copy(e, a).wait_recv()
        early = places(e)[0]
        d = jnp.where(early, decays(tp, a), decays(tt, a))

        def one(m, rows):
            mine = fbuf[e, a, core, rows, :].astype(F32)
            other = fpart[e, a, rows, :].astype(F32)
            comp[e, a, rows, :] = (
                jnp.where(early, other, mine) + d[m:m + 1, :] * jnp.where(early, mine, other)).astype(BF16)

        each_head(one)
        x_copy(e, a).start()

    def row_term(e, a):
        x_copy(e, a).wait_recv()
        _, early, first = places(e)
        d = jnp.where(early, decays(cx, a), decays(csum, a))

        def one(m, rows):
            mine = comp[e, a, rows, :].astype(F32)
            other = xr[e, a, rows, :].astype(F32)
            yt[e, a, rows, :] = (
                jnp.where(early, other, mine) + d[m:m + 1, :] * jnp.where(early, mine, other)).astype(BF16)

        each_head(one)

        @pl.when(first)
        def _():
            y_copy(e, a).start()

    def enter(e, a):
        ahead, early, first = places(e)

        @pl.when(first)
        def _():
            yr[e, a] = jnp.zeros(yr.shape[2:], BF16)

        @pl.when(jnp.logical_not(first))
        def _():
            y_copy(e, a).wait_recv()

        d_row = jnp.where(early, 1.0, decays(cx, a))
        d_core = jnp.where(ahead, decays(tt, a), decays(tp, a))

        def one(m, rows):
            before = jnp.where(early, 0.0, xr[e, a, rows, :].astype(F32))
            reach = before + d_row[m:m + 1, :] * yr[e, a, rows, :].astype(F32)
            mine = fbuf[e, a, core, rows, :].astype(F32)
            other = fpart[e, a, rows, :].astype(F32)
            past = d_core[m:m + 1, :] * reach + jnp.where(ahead, mine, other)
            st[e, a, core, rows, :] = jnp.where(ahead, reach, past).astype(BF16)
            give[e, a, rows, :] = jnp.where(ahead, past, reach).astype(BF16)

        each_head(one)
        s_copy(e, a).start()

    for u in quarters:
        fresh(0, u, ysc, c2)
        f_copy(0, u).start()
    staged[3].wait()
    choose(ball, b2)
    for g in range(groups):
        gmat[g] = dot_nt(c2[g], b2[g])
    tcore.wait_recv()
    csum[...] = tt[...] + tp[...]
    tchip = remote(csum, cx, tsend.at[1], trecv.at[1], 2)
    tchip.start()
    for u in quarters:
        chip_term(0, u)
    for sub in range(1, 4):
        w_send(0, 2, 1, 0, 2, sub)
    w_wait(2, 0, 0, 2)
    w_send(2, 3, 0, 0, 1)
    w_wait(4, 0, 1, 4)
    w_send(4, 5, 0, 1, 1)

    def back_pair(i, carry):
        cols = columns_of(i)
        grad = xg[:, cols]
        low = grad.astype(BF16)
        pe = pexp[i]
        scores = gmat[i // per_group]
        acc = []
        for k in range(2):
            later = pe[:, HEAD_DIM * k:HEAD_DIM * k + 1]
            earlier = prow[i, k:k + 1, :]
            factors = jnp.exp(jnp.where(causal, later - earlier, -1e30))
            w = (scores * factors).astype(BF16)
            wts[2 * i + k] = w
            acc.append(dot_tn(w, low))
        xg[:, cols] = jnp.where(left, acc[0], acc[1]) + gain[i, 0:1, :] * grad
        return carry

    lax.fori_loop(0, pairs, back_pair, 0)
    tchip.wait_recv()
    for u in quarters:
        row_term(0, u)
    w_send(0, 4, 0, 0, 4)
    w_send(0, 2, 0, 1, 2)

    def shard_of(slot):
        return inputs[:, pl.ds(pl.multiple_of(peer(slot) * depth, depth), depth)]

    def x_part(slots, a):
        def one(q, carry):
            cs = pl.ds(pl.multiple_of(q * 512, 512), 512)
            total = dot_nn(shard_of(slots[0]), wbuf[slots[0], a, :, cs])
            for slot in slots[1:]:
                total += dot_nn(shard_of(slot), wbuf[slot, a, :, cs])
            into = pl.ds(pl.multiple_of(a * wide + q * 512, 512), 512)
            if slots[0] == 0:
                xacc[:, into] = total
            else:
                xacc[:, into] += total
            return carry

        lax.fori_loop(0, wide // 512, one, 0)

    def route(i):
        target = peer_dyn(jnp.minimum(i // 2, 6)) // 2
        up = (z + RUNS - 1 - target) // RUNS
        return target, up, up * (RUNS - 1)

    def rcopy(i, up):
        return pltpu.make_async_remote_copy(
            src_ref=pbuf.at[i], dst_ref=rin.at[up, i - 12],
            send_sem=rsend.at[i], recv_sem=rrecv.at[up, i - 12],
            device_id={"head": (z + 1 + up * 2) % RUNS}, device_id_type=pl.DeviceIdType.MESH)

    def dcopy(i, source, target):
        return pltpu.make_async_remote_copy(
            src_ref=pbuf.at[i], dst_ref=rdir.at[source, i % 4],
            send_sem=rsend.at[i], recv_sem=rdrecv.at[source, i % 4],
            device_id={"head": target}, device_id_type=pl.DeviceIdType.MESH)

    def p_send(i, total, far):
        target, up, edge = route(i)
        pbuf[i] = total.astype(BF16)
        if far:
            @pl.when((target != z) & (z == edge))
            def _():
                rcopy(i, up).start()
        else:
            @pl.when(target != z)
            def _():
                dcopy(i, z, target).start()

    def p_some(count, index, far):
        def one(k, carry):
            i = index(k)
            slot, h = i // 2, i % 2
            rows = pl.ds(pl.multiple_of(h * half, half), half)
            total = dot_nt(xg16[:, 0:wide], wbuf[slot, 0, rows, :]) + dot_nt(xg16[:, wide:2 * wide], wbuf[slot, 1, rows, :])
            p_send(i, total, far)
            return carry

        lax.fori_loop(0, count, one, 0)

    def p_diag(sub):
        def picked(a):
            return jnp.concatenate([
                wbuf[slot, a, h * half + sub * fine:h * half + (sub + 1) * fine, :]
                for slot in (6, 7) for h in range(2)], axis=0)

        total = dot_nt(xg16[:, 0:wide], picked(0)) + dot_nt(xg16[:, wide:2 * wide], picked(1))
        p_send(12 + sub, total, True)

    def p_pass(hop, i):
        target, up, edge = route(i)
        away = jnp.where(up == 1, edge - z, z - edge)

        @pl.when((target != z) & (away == hop))
        def _():
            rcopy(i, up).wait_recv()
            pbuf[i] = (pbuf[i].astype(F32) + rin[up, i - 12].astype(F32)).astype(BF16)
            rcopy(i, up).start()

    def group_1(k):
        return 4 + 2 * k + k // 2

    def group_2(k):
        return 5 + 2 * k - k // 2

    def state_of(e, i):
        return st[e, i // 4, (i // 2) % 2, pl.ds(pl.multiple_of((i % 2) * 128, 128), 128), :]

    staged[4].wait()
    for a in range(2):
        own[a].wait()
        for h in range(2):
            w_wait(1, a, h, 1)
        x_part((0, 1), a)

    def z_factor(i, carry):
        cols = columns_of(i)
        gate = gz[:, cols].astype(F32)
        sigma = jax.nn.sigmoid(gate)
        zfac[:, cols] = go[:, cols].astype(F32) * sigma * (1.0 + gate * (1.0 - sigma))
        return carry

    lax.fori_loop(0, pairs, z_factor, 0)
    w_wait(4, 1, 1, 4)
    w_send(4, 5, 1, 1, 1)
    for sub in range(4):
        w_wait(2, 1, 0, 2, sub)
    w_send(2, 3, 1, 0, 1)
    w_send(0, 2, 1, 1, 2)
    w_send(0, 4, 1, 0, 4)
    for u in quarters:
        enter(0, u)
    for u in quarters:
        s_arrival(0, u).wait_recv()

    def back_finish(i, carry):
        cols = columns_of(i)
        pe = pexp[i]
        tail = jnp.exp(pe[SPAN - 1:SPAN, :] - pe)
        xg16[:, cols] = (xg[:, cols] + tail * dot_nt(b2[i // per_group], state_of(0, i))).astype(BF16)
        return carry

    lax.fori_loop(0, pairs, back_finish, 0)
    p_some(4, lambda k: k, False)
    w_wait(3, 0, 0, 1)
    w_wait(5, 0, 1, 1)
    w_wait(3, 1, 0, 1)
    w_wait(5, 1, 1, 1)
    p_some(4, group_1, False)
    w_wait(2, 0, 1, 2)
    w_send(2, 3, 0, 1, 1)
    w_send(2, 6, 0, 0, 4)
    w_wait(4, 0, 0, 4)
    w_send(4, 5, 0, 0, 1)
    w_send(4, 6, 0, 1, 2)
    x_part((2, 4), 0)
    w_wait(3, 0, 1, 1)
    w_wait(5, 0, 0, 1)
    x_part((3, 5), 0)

    def fore_scale(u):
        def one(i, carry):
            cols = columns_of(i)
            x = xacc[:, cols].astype(BF16)
            x16[:, cols] = x
            pe = pexp[i]
            ysc[:, cols] = (x.astype(F32) * jnp.exp(pe[SPAN - 1:SPAN, :] - pe)).astype(BF16)
            return carry

        lax.fori_loop(pairs // 4 * u, pairs // 4 * (u + 1), one, 0)

    def fore_local(u):
        def one(i, carry):
            cols = columns_of(i)
            x = x16[:, cols]
            y = jnp.where(left, dot_nn(wts[2 * i], x), dot_nn(wts[2 * i + 1], x))
            xacc[:, cols] = y + gain[i, 0:1, :] * x.astype(F32)
            return carry

        lax.fori_loop(pairs // 4 * u, pairs // 4 * (u + 1), one, 0)

    def fore_finish(u):
        def one(i, carry):
            cols = columns_of(i)
            y = xacc[:, cols] + jnp.exp(pexp[i]) * dot_nt(c2[i // per_group], state_of(1, i))
            zg_ref[:, cols] = (y * zfac[:, cols]).astype(BF16)
            return carry

        lax.fori_loop(pairs // 4 * u, pairs // 4 * (u + 1), one, 0)

    def own_chunk(i, carry):
        owner = peer_dyn(i // 2)

        @pl.when(owner // 2 == z)
        def _():
            total = pbuf[i].astype(F32)
            for dz in range(1, RUNS):
                source = (z + dz) % RUNS
                dcopy(i, source, source).wait_recv()
                total += rdir[source, i % 4].astype(F32)
            piece = (owner % 2) * 2 + i % 2
            out_ref[:, pl.ds(pl.multiple_of(piece * 256, 256), 256)] = total.astype(BF16)

        return carry

    def own_far():
        @pl.when(peer(6) // 2 == z)
        def _():
            for sub in range(4):
                i = 12 + sub
                cols = slice(sub * 256, (sub + 1) * 256)
                xg[:, cols] = pbuf[i].astype(F32)

                @pl.when(z != 0)
                def _():
                    rcopy(i, 0).wait_recv()
                    xg[:, cols] += rin[0, sub].astype(F32)

                @pl.when(z != RUNS - 1)
                def _():
                    rcopy(i, 1).wait_recv()
                    xg[:, cols] += rin[1, sub].astype(F32)

            for slot in (6, 7):
                for h in range(2):
                    for k in range(2):
                        first = (slot - 6) * 128 + h * 64
                        block = jnp.concatenate([
                            xg[:, sub * 256 + first:sub * 256 + first + 64] for sub in (2 * k, 2 * k + 1)], axis=1)
                        place = (peer(slot) % 2) * 4 + h * 2 + k
                        out_ref[:, pl.ds(pl.multiple_of(place * 128, 128), 128)] = block.astype(BF16)

    w_wait(2, 1, 1, 2)
    w_send(2, 3, 1, 1, 1)
    w_wait(4, 1, 0, 4)
    w_send(4, 5, 1, 0, 1)
    for sub in range(4):
        w_send(4, 6, 1, 1, 2, sub)
        w_send(2, 6, 1, 0, 4, sub)
    x_part((2, 4), 1)
    w_wait(3, 1, 1, 1)
    w_wait(5, 1, 0, 1)
    p_some(4, group_2, False)
    x_part((3, 5), 1)
    w_wait(6, 0, 0, 4)
    w_send(6, 7, 0, 0, 1)
    w_wait(6, 0, 1, 2)
    w_send(6, 7, 0, 1, 1)
    x_part((6,), 0)
    w_wait(7, 0, 0, 1)
    w_wait(7, 0, 1, 1)
    x_part((7,), 0)
    for u in range(2):
        fore_scale(u)
        fresh(1, u, ysc, b2)
        f_copy(1, u).start()
    for u in range(2):
        chip_term(1, u)

    def diag_step(sub):
        w_wait(6, 1, 0, 4, sub)
        w_send(6, 7, 1, 0, 1, sub)
        w_wait(6, 1, 1, 2, sub)
        w_send(6, 7, 1, 1, 1, sub)

    def diag_rest(sub):
        w_wait(7, 1, 0, 1, sub)
        w_wait(7, 1, 1, 1, sub)

    diag_step(0)
    diag_rest(0)
    p_diag(0)
    diag_step(1)
    diag_rest(1)
    p_diag(1)
    for u in range(2):
        fore_local(u)
    diag_step(2)
    p_pass(1, 12)
    diag_rest(2)
    p_diag(2)
    diag_step(3)
    x_part((6,), 1)
    diag_rest(3)
    p_diag(3)
    x_part((7,), 1)
    p_pass(1, 13)
    for u in range(2, 4):
        fore_scale(u)
        fresh(1, u, ysc, b2)
        f_copy(1, u).start()
    p_pass(2, 12)
    p_pass(1, 14)
    for u in range(2, 4):
        chip_term(1, u)
    for u in range(2):
        row_term(1, u)
    p_pass(2, 13)
    p_pass(1, 15)
    for u in range(2, 4):
        fore_local(u)
    p_pass(2, 14)
    for u in range(2):
        enter(1, u)
    for u in range(2, 4):
        row_term(1, u)
    p_pass(2, 15)
    for u in range(2):
        s_arrival(1, u).wait_recv()
        fore_finish(u)
    for u in range(2, 4):
        enter(1, u)
    for u in range(2, 4):
        s_arrival(1, u).wait_recv()
        fore_finish(u)
    lax.fori_loop(0, 12, own_chunk, 0)
    own_far()

    def drain(i, carry):
        target = route(i)[0]

        @pl.when(target != z)
        def _():
            dcopy(i, z, target).wait_send()

        return carry

    lax.fori_loop(0, 16, drain, 0)
    for cp in sent:
        cp.wait_send()
    tcore.wait_send()
    tchip.wait_send()
    for e in range(2):
        for u in quarters:
            f_copy(e, u).wait_send()
            x_copy(e, u).wait_send()
            s_copy(e, u).wait_send()

            @pl.when(places(e)[2])
            def _():
                y_copy(e, u).wait_send()


def fused_body(inputs, x_weight, b_values, c_values, gate_z, log_decay, skip_gain, grad_out):
    heads = log_decay.shape[1]
    width = x_weight.shape[1]
    depth = x_weight.shape[0]
    pairs = heads // 2
    groups = heads * GROUPS // HEADS
    tokens = inputs.shape[0]
    b_rows = b_values.reshape(tokens * GROUPS, STATE)
    c_rows = c_values.reshape(tokens * GROUPS, STATE)
    vmem = pl.BlockSpec(memory_space=pltpu.VMEM)
    hbm = pl.BlockSpec(memory_space=pl.ANY)
    dma = pltpu.SemaphoreType.DMA
    part = pltpu.VMEM((2, 4, heads // 8 * HEAD_DIM, STATE), BF16)
    parts = pltpu.VMEM((2, 4, 2, heads // 8 * HEAD_DIM, STATE), BF16)
    total = pltpu.VMEM((heads, 128), F32)
    return tuple(pl.pallas_call(
        mixer_kernel,
        out_shape=(
            pltpu.VMEM((tokens, inputs.shape[1] // RUNS), BF16),
            pltpu.VMEM((tokens, width), BF16),
        ),
        in_specs=[hbm, hbm, hbm, hbm, hbm, hbm, vmem, vmem],
        out_specs=(vmem, vmem),
        scratch_shapes=[
            pltpu.VMEM(inputs.shape, BF16),
            pltpu.VMEM((tokens, width), BF16),
            pltpu.VMEM((tokens, width), BF16),
            pltpu.VMEM(b_rows.shape, BF16),
            pltpu.VMEM(b_rows.shape, BF16),
            pltpu.VMEM((groups, SPAN, STATE), BF16),
            pltpu.VMEM((groups, SPAN, STATE), BF16),
            pltpu.VMEM((pairs, SPAN, 128), F32),
            pltpu.VMEM((pairs, 8, SPAN), F32),
            pltpu.VMEM((pairs, 8, 128), F32),
            pltpu.VMEM((SEQ, 2, depth, width // 2), BF16),
            pltpu.VMEM((tokens, width), F32),
            pltpu.VMEM((tokens, width), F32),
            pltpu.VMEM((tokens, width), BF16),
            pltpu.VMEM((tokens, width), BF16),
            pltpu.VMEM((heads, SPAN, SPAN), BF16),
            pltpu.VMEM((groups, SPAN, SPAN), F32),
            pltpu.VMEM((tokens, width), BF16),
            pltpu.VMEM((tokens, width), F32),
            pltpu.VMEM((2 * SEQ, tokens, depth // 2), BF16),
            pltpu.VMEM((2, 4, tokens, depth // 2), BF16),
            pltpu.VMEM((RUNS, 4, tokens, depth // 2), BF16),
            parts, part, part, part, part, part, parts, part,
            total, total, total, total,
            dma((5,)), dma((SEQ, 2, 2, 4)), dma((SEQ, 2, 2, 4)), dma((2,)),
            dma((2,)), dma((2,)),
            dma((4, 2, 4)), dma((4, 2, 4)),
            dma((2 * SEQ,)), dma((2, 4)), dma((RUNS, 4)),
        ],
        compiler_params=pltpu.CompilerParams(
            collective_id=0, has_side_effects=True, vmem_limit_bytes=60 * 1024 * 1024),
        name="mixer",
    )(inputs, x_weight, b_rows, c_rows, gate_z, grad_out, log_decay.T, skip_gain[None, :]))


def solution(mesh):
    in_specs = (
        P("seq", None),
        P("seq", "head"),
        P("seq", None, None),
        P("seq", None, None),
        P("seq", "head"),
        P("seq", "head"),
        P("head"),
        P("seq", "head"),
    )
    out_specs = (P("seq", "head"), P("seq", "head"))
    small = mesh.shape["seq"] == SEQ and mesh.shape["head"] == RUNS
    chosen = fused_body if small else body
    return jax.shard_map(chosen, mesh=mesh, in_specs=in_specs, out_specs=out_specs, check_vma=False)
```

```python
import jax
import jax.numpy as jnp
from jax import lax
from jax.sharding import PartitionSpec as P
from jax.experimental import pallas as pl
from jax.experimental.pallas import tpu as pltpu

HEADS = 128
HEAD_DIM = 64
STATE = 128
GROUPS = 8
SPAN = 256


EXACT_MODE = lax.Precision.HIGHEST


def prefix_2(array, axis, combine, identity):
    size, place = (lax.axis_size(axis), lax.axis_index(axis))
    everything = jax.tree.map(
        lambda part, kind: lax.all_gather(part.astype(kind), axis),
        array,
        (jnp.bfloat16, jnp.bfloat16),
    )
    start = jax.tree.map(
        lambda part, zero: jnp.broadcast_to(jnp.asarray(zero, part.dtype), part.shape),
        array,
        identity,
    )

    def prefix_hop(k, before):
        reached = k < place
        new = combine(
            before, jax.tree.map(lambda part, own: part[k].astype(own.dtype), everything, array)
        )
        return jax.tree.map(lambda a, b: jnp.where(reached, a, b), new, before)

    return lax.fori_loop(0, size, prefix_hop, start)


def entering(value, axis, join, neutral):
    count, mine = (lax.axis_size(axis), lax.axis_index(axis))
    pieces = jax.tree.map(lambda part: lax.all_gather(part, axis), value)
    pieces = jax.tree.map(lambda part: part[::-1], pieces)
    mine = count - 1 - mine
    so_far = jax.tree.map(
        lambda part, zero: jnp.full_like(part, 0) + jnp.asarray(zero, part.dtype), value, neutral
    )

    def entering_hop(position, so_far):
        longer = join(so_far, jax.tree.map(lambda part: part[position], pieces))
        return jax.tree.map(lambda new, old: jnp.where(position < mine, new, old), longer, so_far)

    return lax.fori_loop(0, count - 1, entering_hop, so_far)


def decayed_scores(c_block, b_block, prefix):
    scores = jnp.einsum("thn,shn->hts", c_block, b_block, preferred_element_type=jnp.float32)
    later = prefix.T[:, :, None]
    earlier = prefix.T[:, None, :]
    positions = jnp.arange(prefix.shape[0])
    causal = (positions[:, None] >= positions[None, :])[None, :, :]
    spacing = jnp.where(causal, later - earlier, 0.0)
    factors = jnp.where(causal, jnp.exp(spacing), 0.0)
    return (scores * factors).astype(jnp.bfloat16)


def compose(earlier, later):
    return (earlier[0] * later[0], later[0][:, None, None] * earlier[1] + later[1])


def body(inputs, x_weight, b_values, c_values, gate_z, log_decay, skip_gain, grad_out):
    token_count = inputs.shape[0]
    head_count = log_decay.shape[1]
    width_here = x_weight.shape[1]
    block_count = token_count // SPAN
    full_weight = lax.all_gather(x_weight, "seq", axis=0, tiled=True)
    x_sums = jnp.dot(inputs, full_weight, preferred_element_type=jnp.float32)
    x_values = x_sums.astype(jnp.bfloat16)
    first_head = lax.axis_index("head") * head_count
    owners = (first_head + jnp.arange(head_count)) // (HEADS // GROUPS)
    picker = (owners[:, None] == jnp.arange(GROUPS)[None, :]).astype(jnp.bfloat16)
    b_heads = jnp.einsum(
        "tgn,hg->thn", b_values, picker, preferred_element_type=jnp.float32
    ).astype(jnp.bfloat16)
    c_heads = jnp.einsum(
        "tgn,hg->thn", c_values, picker, preferred_element_type=jnp.float32
    ).astype(jnp.bfloat16)
    x_blocks = x_values.reshape(block_count, SPAN, head_count, HEAD_DIM)
    b_blocks = b_heads.reshape(block_count, SPAN, head_count, STATE)
    c_blocks = c_heads.reshape(block_count, SPAN, head_count, STATE)
    spots = jnp.arange(SPAN)
    so_far = (spots[:, None] >= spots[None, :]).astype(jnp.float32)
    prefix = jnp.einsum(
        "tr,krh->kth", so_far, log_decay.reshape(block_count, SPAN, head_count), precision=EXACT_MODE
    )
    totals = prefix[:, -1, :]
    gate = gate_z.astype(jnp.float32).reshape(token_count, head_count, HEAD_DIM)
    upstream = grad_out.astype(jnp.float32).reshape(token_count, head_count, HEAD_DIM)
    sigma = jax.nn.sigmoid(gate)
    y_grad = upstream * gate * sigma
    grad_blocks = y_grad.reshape(block_count, SPAN, head_count, HEAD_DIM)
    low_blocks = grad_blocks.astype(jnp.bfloat16)
    tails = jnp.exp(totals[:, None, :] - prefix)
    fresh_states = jnp.einsum(
        "kshp,kshn->khpn",
        x_blocks.astype(jnp.float32) * tails[..., None],
        b_blocks.astype(jnp.float32),
        precision=EXACT_MODE,
    )
    fresh_grads = jnp.einsum(
        "kthp,kthn->khpn",
        grad_blocks * jnp.exp(prefix)[..., None],
        c_blocks.astype(jnp.float32),
        precision=EXACT_MODE,
    )
    blocks = jnp.arange(block_count)
    up_to = (blocks[:, None] >= blocks[None, :]).astype(jnp.float32)
    running = jnp.einsum("jk,kh->jh", up_to, totals, precision=EXACT_MODE)
    after = running[-1][None, :] - running
    before = running - totals
    device_decay = jnp.exp(running[-1])
    device_state = jnp.einsum("kh,khpn->hpn", jnp.exp(after), fresh_states, precision=EXACT_MODE)
    device_grad = jnp.einsum("kh,khpn->hpn", jnp.exp(before), fresh_grads, precision=EXACT_MODE)
    unit_decay = jnp.ones((head_count,), jnp.float32)
    start_state = prefix_2(
        (device_decay, device_state), "seq", compose, (unit_decay, jnp.zeros_like(device_state))
    )[1]
    end_grad = entering(
        (device_decay, device_grad), "seq", compose, (unit_decay, jnp.zeros_like(device_grad))
    )[1]
    gain = skip_gain[None, :, None]

    def forward(state, items):
        x_block, b_block, c_block, prefix_block, fresh = items
        weights = decayed_scores(c_block, b_block, prefix_block)
        local = jnp.einsum("hts,shp->thp", weights, x_block, preferred_element_type=jnp.float32)
        carried = jnp.exp(prefix_block)[:, :, None] * jnp.einsum(
            "thn,hpn->thp", c_block.astype(jnp.float32), state, precision=EXACT_MODE
        )
        state = jnp.exp(prefix_block[-1])[:, None, None] * state + fresh
        return (state, (local + carried + gain * x_block.astype(jnp.float32), weights))

    final_state, (outputs, weight_blocks) = lax.scan(
        forward, start_state, (x_blocks, b_blocks, c_blocks, prefix, fresh_states)
    )
    outputs = outputs.reshape(token_count, head_count, HEAD_DIM)
    z_grad = (upstream * outputs * sigma * (1.0 + gate * (1.0 - sigma))).astype(jnp.bfloat16)
    z_grad = z_grad.reshape(token_count, width_here)

    def backward(carry, items):
        weights, b_block, tail_block, total_block, grad_block, low_block, fresh = items
        local = jnp.einsum("hts,thp->shp", weights, low_block, preferred_element_type=jnp.float32)
        carried = tail_block[:, :, None] * jnp.einsum(
            "shn,hpn->shp", b_block.astype(jnp.float32), carry, precision=EXACT_MODE
        )
        carry = jnp.exp(total_block)[:, None, None] * carry + fresh
        return (carry, local + carried + gain * grad_block)

    final_grad, x_grads = lax.scan(
        backward,
        end_grad,
        (weight_blocks, b_blocks, tails, totals, grad_blocks, low_blocks, fresh_grads),
        reverse=True,
    )
    x_grad = x_grads.reshape(token_count, width_here).astype(jnp.bfloat16)
    partial_sums = jnp.einsum("tk,dk->td", x_grad, full_weight, preferred_element_type=jnp.float32)
    input_grad = lax.psum_scatter(
        partial_sums.astype(jnp.bfloat16), "head", scatter_dimension=1, tiled=True
    )
    return (input_grad, z_grad)


SEQ = 8
RUNS = 4
F32 = jnp.float32
BF16 = jnp.bfloat16


def dot_nn(a, b):
    return lax.dot_general(a, b, (((1,), (0,)), ((), ())), preferred_element_type=F32)


def dot_nt(a, b):
    return lax.dot_general(a, b, (((1,), (1,)), ((), ())), preferred_element_type=F32)


def dot_tn(a, b):
    return lax.dot_general(a, b, (((0,), (0,)), ((), ())), preferred_element_type=F32)


def exact_nn(a, b):
    return lax.dot_general(a, b, (((1,), (0,)), ((), ())), preferred_element_type=F32, precision=EXACT_MODE)


def exact_nt(a, b):
    return lax.dot_general(a, b, (((1,), (1,)), ((), ())), preferred_element_type=F32, precision=EXACT_MODE)


def mixer_kernel(
    in_hbm, w_hbm, b_hbm, c_hbm, gz_hbm, go_hbm, decay_ref, skip_ref,
    out_ref, zg_ref,
    inputs, gz, go, ball, call, b2, c2, pexp, prow, gain,
    wbuf, xacc, xg, xg16, ysc, wts, gmat, x16, zfac, pbuf, rin, rdir,
    fbuf, fpart, comp, xr, yt, yr, st, give, tt, tp, csum, cx,
    loads, wsend, wrecv, wlocal, tsend, trecv, esend, erecv, rsend, rrecv, rdrecv,
):
    s = lax.axis_index("seq")
    z = lax.axis_index("head")
    core, xx, yy = s % 2, (s // 2) % 2, s // 4
    depth = w_hbm.shape[0]
    half = depth // 2
    fine = half // 4
    wide = w_hbm.shape[1] // 2
    heads = wts.shape[0]
    pairs = heads // 2
    groups = b2.shape[0]
    per_group = pairs // groups
    per = heads // 8
    quarters = range(4)

    def peer(r):
        a = (1 - core) if r & 1 else core
        b = (1 - xx) if r & 2 else xx
        c = (1 - yy) if r & 4 else yy
        return c * 4 + b * 2 + a

    def peer_dyn(r):
        a = (core + r) % 2
        b = (xx + r // 2) % 2
        c = (yy + r // 4) % 2
        return c * 4 + b * 2 + a

    def remote(src, dst, ssem, rsem, to):
        return pltpu.make_async_remote_copy(
            src_ref=src, dst_ref=dst, send_sem=ssem, recv_sem=rsem,
            device_id={"seq": peer(to)}, device_id_type=pl.DeviceIdType.MESH)

    staged = [pltpu.make_async_copy(src, dst, loads.at[n]) for n, (src, dst) in enumerate(
        ((gz_hbm, gz), (go_hbm, go), (c_hbm, call), (b_hbm, ball), (in_hbm, inputs)))]
    for cp in staged:
        cp.start()
    barrier = pltpu.get_barrier_semaphore()
    for r in (1, 2, 4):
        pl.semaphore_signal(barrier, inc=1, device_id={"seq": peer(r)}, device_id_type=pl.DeviceIdType.MESH)
    for dz in range(1, RUNS):
        pl.semaphore_signal(barrier, inc=1, device_id={"head": (z + dz) % RUNS}, device_id_type=pl.DeviceIdType.MESH)
    pl.semaphore_wait(barrier, 3 + RUNS - 1)

    def rows_of(h, sub):
        if sub is None:
            return pl.ds(h * half, half)
        return pl.ds(h * half + sub * fine, fine)

    def wcopy(src_slot, dst_slot, a, h, to, sub=None):
        rows = rows_of(h, sub)
        if src_slot == 0:
            src = w_hbm.at[rows, pl.ds(a * wide, wide)]
        else:
            src = wbuf.at[src_slot, a, rows, :]
        return remote(src, wbuf.at[dst_slot, a, rows, :],
                      wsend.at[dst_slot, a, h, sub or 0], wrecv.at[dst_slot, a, h, sub or 0], to)

    own = [pltpu.make_async_copy(w_hbm.at[:, pl.ds(a * wide, wide)], wbuf.at[0, a], wlocal.at[a]) for a in range(2)]
    sent = []

    def w_send(src_slot, dst_slot, a, h, to, sub=None):
        cp = wcopy(src_slot, dst_slot, a, h, to, sub)
        cp.start()
        sent.append(cp)

    def w_wait(slot, a, h, to, sub=None):
        wcopy(0, slot, a, h, to, sub).wait_recv()

    w_send(0, 2, 0, 0, 2)
    w_send(0, 4, 0, 1, 4)
    w_send(0, 2, 1, 0, 2, 0)
    w_send(0, 4, 1, 1, 4)
    for cp in own:
        cp.start()
    for a in range(2):
        for h in range(2):
            w_send(0, 1, a, h, 1)

    lower = (lax.broadcasted_iota(jnp.int32, (SPAN, SPAN), 0) >= lax.broadcasted_iota(jnp.int32, (SPAN, SPAN), 1))
    ones = jnp.where(lower, 1.0, 0.0).astype(F32)
    prefix = exact_nt(ones, decay_ref[...])
    across = exact_nt(decay_ref[...], ones)
    tt[...] = jnp.broadcast_to(across[:, SPAN - 1:SPAN], (heads, 128))
    tcore = remote(tt, tp, tsend.at[0], trecv.at[0], 1)
    tcore.start()
    for i in range(pairs):
        prow[i, 0:2, :] = across[2 * i:2 * i + 2, :]
    both = jnp.concatenate([prefix, jnp.broadcast_to(skip_ref[...], (8, heads))], axis=0)

    lanes = lax.broadcasted_iota(jnp.int32, (SPAN, 128), 1)
    left = lanes < HEAD_DIM
    causal = lax.broadcasted_iota(jnp.int32, (SPAN, SPAN), 0) >= lax.broadcasted_iota(jnp.int32, (SPAN, SPAN), 1)

    def columns_of(i):
        return pl.ds(pl.multiple_of(i * 128, 128), 128)

    staged[0].wait()
    staged[1].wait()

    def prepare_pair(i, carry):
        cols = columns_of(i)
        head = lax.broadcasted_iota(jnp.int32, (heads, 128), 0)
        lane = lax.broadcasted_iota(jnp.int32, (heads, 128), 1)
        pick = jnp.where(head == 2 * i + lane // HEAD_DIM, 1.0, 0.0).astype(F32)
        spread = exact_nn(both, pick)
        pe = spread[:SPAN]
        pexp[i] = pe
        gain[i] = spread[SPAN:]
        gate = gz[:, cols].astype(F32)
        grad = go[:, cols].astype(F32) * gate * jax.nn.sigmoid(gate)
        xg[:, cols] = grad
        ysc[:, cols] = (grad * jnp.exp(pe)).astype(BF16)
        return carry

    lax.fori_loop(0, pairs, prepare_pair, 0)

    some = SPAN // GROUPS
    row = lax.broadcasted_iota(jnp.int32, (groups * some, SPAN), 0)
    col = lax.broadcasted_iota(jnp.int32, (groups * some, SPAN), 1)
    chooser = jnp.where(col == (row % some) * GROUPS + z * groups + row // some, 1.0, 0.0).astype(BF16)

    def choose(src, dst):
        def one(k, carry):
            block = src[pl.ds(pl.multiple_of(k * SPAN, SPAN), SPAN), :]
            chosen = dot_nn(chooser, block).astype(BF16)
            for g in range(groups):
                dst[g, pl.ds(pl.multiple_of(k * some, some), some), :] = chosen[g * some:(g + 1) * some]
            return carry

        lax.fori_loop(0, GROUPS, one, 0)

    staged[2].wait()
    choose(call, c2)

    def fresh(e, u, src, maps):
        def one(j, carry):
            cols = pl.ds(pl.multiple_of(j * 256, 256), 256)
            fbuf[e, u, j % 2] = dot_tn(src[:, cols], maps[j // (SEQ // groups)]).astype(BF16)
            return carry

        lax.fori_loop(2 * u, 2 * u + 2, one, 0)

    def f_copy(e, a):
        return remote(fbuf.at[e, a, 1 - core], fpart.at[e, a], esend.at[0, e, a], erecv.at[0, e, a], 1)

    def x_copy(e, a):
        return remote(comp.at[e, a], xr.at[e, a], esend.at[1, e, a], erecv.at[1, e, a], 2)

    def y_copy(e, a):
        return remote(yt.at[e, a], yr.at[e, a], esend.at[2, e, a], erecv.at[2, e, a], 4)

    def s_copy(e, a):
        return remote(give.at[e, a], st.at[e, a, core], esend.at[3, e, a], erecv.at[3, e, a], 1)

    def s_arrival(e, a):
        return remote(give.at[e, a], st.at[e, a, 1 - core], esend.at[3, e, a], erecv.at[3, e, a], 1)

    def places(e):
        if e == 1:
            return core == 0, xx == 0, yy == 0
        return core == 1, xx == 1, yy == 1

    def decays(ref, a):
        both_cores = ref[a * 2 * per:(a + 1) * 2 * per, :]
        return jnp.exp(jnp.where(core == 0, both_cores[:per], both_cores[per:]))

    def each_head(one):
        for m in range(per):
            one(m, slice(m * HEAD_DIM, (m + 1) * HEAD_DIM))

    def chip_term(e, a):
        f_copy(e, a).wait_recv()
        early = places(e)[0]
        d = jnp.where(early, decays(tp, a), decays(tt, a))

        def one(m, rows):
            mine = fbuf[e, a, core, rows, :].astype(F32)
            other = fpart[e, a, rows, :].astype(F32)
            comp[e, a, rows, :] = (
                jnp.where(early, other, mine) + d[m:m + 1, :] * jnp.where(early, mine, other)).astype(BF16)

        each_head(one)
        x_copy(e, a).start()

    def row_term(e, a):
        x_copy(e, a).wait_recv()
        _, early, first = places(e)
        d = jnp.where(early, decays(cx, a), decays(csum, a))

        def one(m, rows):
            mine = comp[e, a, rows, :].astype(F32)
            other = xr[e, a, rows, :].astype(F32)
            yt[e, a, rows, :] = (
                jnp.where(early, other, mine) + d[m:m + 1, :] * jnp.where(early, mine, other)).astype(BF16)

        each_head(one)

        @pl.when(first)
        def _():
            y_copy(e, a).start()

    def enter(e, a):
        ahead, early, first = places(e)

        @pl.when(first)
        def _():
            yr[e, a] = jnp.zeros(yr.shape[2:], BF16)

        @pl.when(jnp.logical_not(first))
        def _():
            y_copy(e, a).wait_recv()

        d_row = jnp.where(early, 1.0, decays(cx, a))
        d_core = jnp.where(ahead, decays(tt, a), decays(tp, a))

        def one(m, rows):
            before = jnp.where(early, 0.0, xr[e, a, rows, :].astype(F32))
            reach = before + d_row[m:m + 1, :] * yr[e, a, rows, :].astype(F32)
            mine = fbuf[e, a, core, rows, :].astype(F32)
            other = fpart[e, a, rows, :].astype(F32)
            past = d_core[m:m + 1, :] * reach + jnp.where(ahead, mine, other)
            st[e, a, core, rows, :] = jnp.where(ahead, reach, past).astype(BF16)
            give[e, a, rows, :] = jnp.where(ahead, past, reach).astype(BF16)

        each_head(one)
        s_copy(e, a).start()

    for u in quarters:
        fresh(0, u, ysc, c2)
        f_copy(0, u).start()
    staged[3].wait()
    choose(ball, b2)
    for g in range(groups):
        gmat[g] = dot_nt(c2[g], b2[g])
    tcore.wait_recv()
    csum[...] = tt[...] + tp[...]
    tchip = remote(csum, cx, tsend.at[1], trecv.at[1], 2)
    tchip.start()
    for u in quarters:
        chip_term(0, u)
    for sub in range(1, 4):
        w_send(0, 2, 1, 0, 2, sub)
    w_wait(2, 0, 0, 2)
    w_send(2, 3, 0, 0, 1)
    w_wait(4, 0, 1, 4)
    w_send(4, 5, 0, 1, 1)

    def back_pair(i, carry):
        cols = columns_of(i)
        grad = xg[:, cols]
        low = grad.astype(BF16)
        pe = pexp[i]
        scores = gmat[i // per_group]
        acc = []
        for k in range(2):
            later = pe[:, HEAD_DIM * k:HEAD_DIM * k + 1]
            earlier = prow[i, k:k + 1, :]
            factors = jnp.exp(jnp.where(causal, later - earlier, -1e30))
            w = (scores * factors).astype(BF16)
            wts[2 * i + k] = w
            acc.append(dot_tn(w, low))
        xg[:, cols] = jnp.where(left, acc[0], acc[1]) + gain[i, 0:1, :] * grad
        return carry

    lax.fori_loop(0, pairs, back_pair, 0)
    tchip.wait_recv()
    for u in quarters:
        row_term(0, u)
    w_send(0, 4, 0, 0, 4)
    w_send(0, 2, 0, 1, 2)

    def shard_of(slot):
        return inputs[:, pl.ds(pl.multiple_of(peer(slot) * depth, depth), depth)]

    def x_part(slots, a):
        def one(q, carry):
            cs = pl.ds(pl.multiple_of(q * 512, 512), 512)
            total = dot_nn(shard_of(slots[0]), wbuf[slots[0], a, :, cs])
            for slot in slots[1:]:
                total += dot_nn(shard_of(slot), wbuf[slot, a, :, cs])
            into = pl.ds(pl.multiple_of(a * wide + q * 512, 512), 512)
            if slots[0] == 0:
                xacc[:, into] = total
            else:
                xacc[:, into] += total
            return carry

        lax.fori_loop(0, wide // 512, one, 0)

    def route(i):
        target = peer_dyn(jnp.minimum(i // 2, 6)) // 2
        up = (z + RUNS - 1 - target) // RUNS
        return target, up, up * (RUNS - 1)

    def rcopy(i, up):
        return pltpu.make_async_remote_copy(
            src_ref=pbuf.at[i], dst_ref=rin.at[up, i - 12],
            send_sem=rsend.at[i], recv_sem=rrecv.at[up, i - 12],
            device_id={"head": (z + 1 + up * 2) % RUNS}, device_id_type=pl.DeviceIdType.MESH)

    def dcopy(i, source, target):
        return pltpu.make_async_remote_copy(
            src_ref=pbuf.at[i], dst_ref=rdir.at[source, i % 4],
            send_sem=rsend.at[i], recv_sem=rdrecv.at[source, i % 4],
            device_id={"head": target}, device_id_type=pl.DeviceIdType.MESH)

    def p_send(i, total, far):
        target, up, edge = route(i)
        pbuf[i] = total.astype(BF16)
        if far:
            @pl.when((target != z) & (z == edge))
            def _():
                rcopy(i, up).start()
        else:
            @pl.when(target != z)
            def _():
                dcopy(i, z, target).start()

    def p_some(count, index, far):
        def one(k, carry):
            i = index(k)
            slot, h = i // 2, i % 2
            rows = pl.ds(pl.multiple_of(h * half, half), half)
            total = dot_nt(xg16[:, 0:wide], wbuf[slot, 0, rows, :]) + dot_nt(xg16[:, wide:2 * wide], wbuf[slot, 1, rows, :])
            p_send(i, total, far)
            return carry

        lax.fori_loop(0, count, one, 0)

    def p_diag(sub):
        def picked(a):
            return jnp.concatenate([
                wbuf[slot, a, h * half + sub * fine:h * half + (sub + 1) * fine, :]
                for slot in (6, 7) for h in range(2)], axis=0)

        total = dot_nt(xg16[:, 0:wide], picked(0)) + dot_nt(xg16[:, wide:2 * wide], picked(1))
        p_send(12 + sub, total, True)

    def p_pass(hop, i):
        target, up, edge = route(i)
        away = jnp.where(up == 1, edge - z, z - edge)

        @pl.when((target != z) & (away == hop))
        def _():
            rcopy(i, up).wait_recv()
            pbuf[i] = (pbuf[i].astype(F32) + rin[up, i - 12].astype(F32)).astype(BF16)
            rcopy(i, up).start()

    def group_1(k):
        return 4 + 2 * k + k // 2

    def group_2(k):
        return 5 + 2 * k - k // 2

    def state_of(e, i):
        return st[e, i // 4, (i // 2) % 2, pl.ds(pl.multiple_of((i % 2) * 128, 128), 128), :]

    staged[4].wait()
    for a in range(2):
        own[a].wait()
        for h in range(2):
            w_wait(1, a, h, 1)
        x_part((0, 1), a)

    def z_factor(i, carry):
        cols = columns_of(i)
        gate = gz[:, cols].astype(F32)
        sigma = jax.nn.sigmoid(gate)
        zfac[:, cols] = go[:, cols].astype(F32) * sigma * (1.0 + gate * (1.0 - sigma))
        return carry

    lax.fori_loop(0, pairs, z_factor, 0)
    w_wait(4, 1, 1, 4)
    w_send(4, 5, 1, 1, 1)
    for sub in range(4):
        w_wait(2, 1, 0, 2, sub)
    w_send(2, 3, 1, 0, 1)
    w_send(0, 2, 1, 1, 2)
    w_send(0, 4, 1, 0, 4)
    for u in quarters:
        enter(0, u)
    for u in quarters:
        s_arrival(0, u).wait_recv()

    def back_finish(i, carry):
        cols = columns_of(i)
        pe = pexp[i]
        tail = jnp.exp(pe[SPAN - 1:SPAN, :] - pe)
        xg16[:, cols] = (xg[:, cols] + tail * dot_nt(b2[i // per_group], state_of(0, i))).astype(BF16)
        return carry

    lax.fori_loop(0, pairs, back_finish, 0)
    p_some(4, lambda k: k, False)
    w_wait(3, 0, 0, 1)
    w_wait(5, 0, 1, 1)
    w_wait(3, 1, 0, 1)
    w_wait(5, 1, 1, 1)
    p_some(4, group_1, False)
    w_wait(2, 0, 1, 2)
    w_send(2, 3, 0, 1, 1)
    w_send(2, 6, 0, 0, 4)
    w_wait(4, 0, 0, 4)
    w_send(4, 5, 0, 0, 1)
    w_send(4, 6, 0, 1, 2)
    x_part((2, 4), 0)
    w_wait(3, 0, 1, 1)
    w_wait(5, 0, 0, 1)
    x_part((3, 5), 0)

    def fore_scale(u):
        def one(i, carry):
            cols = columns_of(i)
            x = xacc[:, cols].astype(BF16)
            x16[:, cols] = x
            pe = pexp[i]
            ysc[:, cols] = (x.astype(F32) * jnp.exp(pe[SPAN - 1:SPAN, :] - pe)).astype(BF16)
            return carry

        lax.fori_loop(pairs // 4 * u, pairs // 4 * (u + 1), one, 0)

    def fore_local(u):
        def one(i, carry):
            cols = columns_of(i)
            x = x16[:, cols]
            y = jnp.where(left, dot_nn(wts[2 * i], x), dot_nn(wts[2 * i + 1], x))
            xacc[:, cols] = y + gain[i, 0:1, :] * x.astype(F32)
            return carry

        lax.fori_loop(pairs // 4 * u, pairs // 4 * (u + 1), one, 0)

    def fore_finish(u):
        def one(i, carry):
            cols = columns_of(i)
            y = xacc[:, cols] + jnp.exp(pexp[i]) * dot_nt(c2[i // per_group], state_of(1, i))
            zg_ref[:, cols] = (y * zfac[:, cols]).astype(BF16)
            return carry

        lax.fori_loop(pairs // 4 * u, pairs // 4 * (u + 1), one, 0)

    def own_chunk(i, carry):
        owner = peer_dyn(i // 2)

        @pl.when(owner // 2 == z)
        def _():
            total = pbuf[i].astype(F32)
            for dz in range(1, RUNS):
                source = (z + dz) % RUNS
                dcopy(i, source, source).wait_recv()
                total += rdir[source, i % 4].astype(F32)
            piece = (owner % 2) * 2 + i % 2
            out_ref[:, pl.ds(pl.multiple_of(piece * 256, 256), 256)] = total.astype(BF16)

        return carry

    def own_far():
        @pl.when(peer(6) // 2 == z)
        def _():
            for sub in range(4):
                i = 12 + sub
                cols = slice(sub * 256, (sub + 1) * 256)
                xg[:, cols] = pbuf[i].astype(F32)

                @pl.when(z != 0)
                def _():
                    rcopy(i, 0).wait_recv()
                    xg[:, cols] += rin[0, sub].astype(F32)

                @pl.when(z != RUNS - 1)
                def _():
                    rcopy(i, 1).wait_recv()
                    xg[:, cols] += rin[1, sub].astype(F32)

            for slot in (6, 7):
                for h in range(2):
                    for k in range(2):
                        first = (slot - 6) * 128 + h * 64
                        block = jnp.concatenate([
                            xg[:, sub * 256 + first:sub * 256 + first + 64] for sub in (2 * k, 2 * k + 1)], axis=1)
                        place = (peer(slot) % 2) * 4 + h * 2 + k
                        out_ref[:, pl.ds(pl.multiple_of(place * 128, 128), 128)] = block.astype(BF16)

    w_wait(2, 1, 1, 2)
    w_send(2, 3, 1, 1, 1)
    w_wait(4, 1, 0, 4)
    w_send(4, 5, 1, 0, 1)
    for sub in range(4):
        w_send(4, 6, 1, 1, 2, sub)
        w_send(2, 6, 1, 0, 4, sub)
    x_part((2, 4), 1)
    w_wait(3, 1, 1, 1)
    w_wait(5, 1, 0, 1)
    p_some(4, group_2, False)
    x_part((3, 5), 1)
    w_wait(6, 0, 0, 4)
    w_send(6, 7, 0, 0, 1)
    w_wait(6, 0, 1, 2)
    w_send(6, 7, 0, 1, 1)
    x_part((6,), 0)
    w_wait(7, 0, 0, 1)
    w_wait(7, 0, 1, 1)
    x_part((7,), 0)
    for u in range(2):
        fore_scale(u)
        fresh(1, u, ysc, b2)
        f_copy(1, u).start()
    for u in range(2):
        chip_term(1, u)

    def diag_step(sub):
        w_wait(6, 1, 0, 4, sub)
        w_send(6, 7, 1, 0, 1, sub)
        w_wait(6, 1, 1, 2, sub)
        w_send(6, 7, 1, 1, 1, sub)

    def diag_rest(sub):
        w_wait(7, 1, 0, 1, sub)
        w_wait(7, 1, 1, 1, sub)

    diag_step(0)
    diag_rest(0)
    p_diag(0)
    diag_step(1)
    diag_rest(1)
    p_diag(1)
    for u in range(2):
        fore_local(u)
    diag_step(2)
    p_pass(1, 12)
    diag_rest(2)
    p_diag(2)
    diag_step(3)
    x_part((6,), 1)
    diag_rest(3)
    p_diag(3)
    x_part((7,), 1)
    p_pass(1, 13)
    for u in range(2, 4):
        fore_scale(u)
        fresh(1, u, ysc, b2)
        f_copy(1, u).start()
    p_pass(2, 12)
    p_pass(1, 14)
    for u in range(2, 4):
        chip_term(1, u)
    for u in range(2):
        row_term(1, u)
    p_pass(2, 13)
    p_pass(1, 15)
    for u in range(2, 4):
        fore_local(u)
    p_pass(2, 14)
    for u in range(2):
        enter(1, u)
    for u in range(2, 4):
        row_term(1, u)
    p_pass(2, 15)
    for u in range(2):
        s_arrival(1, u).wait_recv()
        fore_finish(u)
    lax.fori_loop(0, 12, own_chunk, 0)
    for u in range(2, 4):
        enter(1, u)
    for u in range(2, 4):
        s_arrival(1, u).wait_recv()
        fore_finish(u)
    own_far()

    def drain(i, carry):
        target = route(i)[0]

        @pl.when(target != z)
        def _():
            dcopy(i, z, target).wait_send()

        return carry

    lax.fori_loop(0, 16, drain, 0)
    for cp in sent:
        cp.wait_send()
    tcore.wait_send()
    tchip.wait_send()
    for e in range(2):
        for u in quarters:
            f_copy(e, u).wait_send()
            x_copy(e, u).wait_send()
            s_copy(e, u).wait_send()

            @pl.when(places(e)[2])
            def _():
                y_copy(e, u).wait_send()


def fused_body(inputs, x_weight, b_values, c_values, gate_z, log_decay, skip_gain, grad_out):
    heads = log_decay.shape[1]
    width = x_weight.shape[1]
    depth = x_weight.shape[0]
    pairs = heads // 2
    groups = heads * GROUPS // HEADS
    tokens = inputs.shape[0]
    b_rows = b_values.reshape(tokens * GROUPS, STATE)
    c_rows = c_values.reshape(tokens * GROUPS, STATE)
    vmem = pl.BlockSpec(memory_space=pltpu.VMEM)
    hbm = pl.BlockSpec(memory_space=pl.ANY)
    dma = pltpu.SemaphoreType.DMA
    part = pltpu.VMEM((2, 4, heads // 8 * HEAD_DIM, STATE), BF16)
    parts = pltpu.VMEM((2, 4, 2, heads // 8 * HEAD_DIM, STATE), BF16)
    total = pltpu.VMEM((heads, 128), F32)
    return tuple(pl.pallas_call(
        mixer_kernel,
        out_shape=(
            pltpu.VMEM((tokens, inputs.shape[1] // RUNS), BF16),
            pltpu.VMEM((tokens, width), BF16),
        ),
        in_specs=[hbm, hbm, hbm, hbm, hbm, hbm, vmem, vmem],
        out_specs=(vmem, vmem),
        scratch_shapes=[
            pltpu.VMEM(inputs.shape, BF16),
            pltpu.VMEM((tokens, width), BF16),
            pltpu.VMEM((tokens, width), BF16),
            pltpu.VMEM(b_rows.shape, BF16),
            pltpu.VMEM(b_rows.shape, BF16),
            pltpu.VMEM((groups, SPAN, STATE), BF16),
            pltpu.VMEM((groups, SPAN, STATE), BF16),
            pltpu.VMEM((pairs, SPAN, 128), F32),
            pltpu.VMEM((pairs, 8, SPAN), F32),
            pltpu.VMEM((pairs, 8, 128), F32),
            pltpu.VMEM((SEQ, 2, depth, width // 2), BF16),
            pltpu.VMEM((tokens, width), F32),
            pltpu.VMEM((tokens, width), F32),
            pltpu.VMEM((tokens, width), BF16),
            pltpu.VMEM((tokens, width), BF16),
            pltpu.VMEM((heads, SPAN, SPAN), BF16),
            pltpu.VMEM((groups, SPAN, SPAN), F32),
            pltpu.VMEM((tokens, width), BF16),
            pltpu.VMEM((tokens, width), F32),
            pltpu.VMEM((2 * SEQ, tokens, depth // 2), BF16),
            pltpu.VMEM((2, 4, tokens, depth // 2), BF16),
            pltpu.VMEM((RUNS, 4, tokens, depth // 2), BF16),
            parts, part, part, part, part, part, parts, part,
            total, total, total, total,
            dma((5,)), dma((SEQ, 2, 2, 4)), dma((SEQ, 2, 2, 4)), dma((2,)),
            dma((2,)), dma((2,)),
            dma((4, 2, 4)), dma((4, 2, 4)),
            dma((2 * SEQ,)), dma((2, 4)), dma((RUNS, 4)),
        ],
        compiler_params=pltpu.CompilerParams(
            collective_id=0, has_side_effects=True, vmem_limit_bytes=60 * 1024 * 1024),
        name="mixer",
    )(inputs, x_weight, b_rows, c_rows, gate_z, grad_out, log_decay.T, skip_gain[None, :]))


def solution(mesh):
    in_specs = (
        P("seq", None),
        P("seq", "head"),
        P("seq", None, None),
        P("seq", None, None),
        P("seq", "head"),
        P("seq", "head"),
        P("head"),
        P("seq", "head"),
    )
    out_specs = (P("seq", "head"), P("seq", "head"))
    small = mesh.shape["seq"] == SEQ and mesh.shape["head"] == RUNS
    chosen = fused_body if small else body
    return jax.shard_map(chosen, mesh=mesh, in_specs=in_specs, out_specs=out_specs, check_vma=False)
```
